128 devices in a mesh: chan: 8 (over z, core), tm: 16 (over y, x).
Axes of the slice: x: 4, y: 4, z: 4, core: 2. Of those that a mesh axis runs over, the one named last changes fastest.
Arguments:
- voltages: bfloat16 [2, 64, 8, 1048576], P(None, 'tm', 'chan'), may hold values from -6 to 6
- antenna_gains: float32 [2, 64, 8], P(None, None, 'chan'), may hold values from -0.75 to 0.75
- chirp_phase: float32 [8, 131072], P('chan'), may hold values from -3.140625 to 3.140625
- offsets: int32 [8], P('chan'), may hold values from 0 to 4095, as said below
- flags: int32 [8, 1024], P('chan', 'tm'), may hold values 0 or 1
- sample_phase_bins: int32 [1048576], P('tm'), may hold values from 0 to 2047
Outputs:
- dedispersed: bfloat16 [2, 8, 1048576], P(None, 'chan', 'tm')
- sk_weight: float32 [8, 1024], P('chan', 'tm')
- profile: float32 [8, 2048], P('chan', 'tm')
- band_profile: float32 [2048], P('tm')
The draws below stay inside these ranges and needn't reach their ends.
Inputs may be any that keep to these rules, and one draw needn't show every extreme that they name: `offsets`: some channel has the offset 4096 - 1.
All inputs are finite; a program needn't handle non-finite values. No bound on the sum of `flags` on one device may be relied on, other than what follows from the above.
Results may differ from the reference program's by a relative error of at most 0.0045.
Values may be sent and summed in bfloat16 or wider, within the bound.
No kernel may reach another device: no remote copies, remote signals or barrier semaphores. Data moves between devices by JAX's collectives and lax.ppermute only.
A program may use at most 192 MiB of HBM per device.

```python
import jax
import jax.numpy as jnp
from jax import lax

ANTENNA_COUNT = 64
NFFT = 131072
OFFSET_BOUND = 4096
SKW = 1024
BINS = 2048
TS = 65536
CHANNEL_COUNT = 8
TIME_SAMPLES = 1048576
NWIN = 1024
N_TM = 16


def draw_offsets(key, part):
    values = jax.random.randint(jax.random.fold_in(key, 11), (CHANNEL_COUNT,), 0, OFFSET_BOUND, dtype=jnp.int32)
    chosen = jax.random.randint(jax.random.fold_in(key, 12), (), 0, CHANNEL_COUNT, dtype=jnp.int32)
    marker = jnp.arange(CHANNEL_COUNT, dtype=jnp.int32) == chosen
    return jnp.where(marker, OFFSET_BOUND - 1, values).astype(jnp.int32)


def place_ends(array, key, smallest, top_value):
    extent = array.shape
    spot = [jax.random.randint(jax.random.fold_in(key, axis), (), 0, extent[axis]) for axis in range(len(extent))]
    array = array.at[tuple(spot)].set(smallest)
    longest = extent.index(max(extent))
    spot[longest] = (spot[longest] + 1) % extent[longest]
    return array.at[tuple(spot)].set(top_value)


def with_spikes(drawn, rng, source, target, blocks, factor):
    def block_of(dim):
        return (jnp.arange(drawn.shape[dim]) // (drawn.shape[dim] // blocks)).reshape((-1,) + (1,) * (drawn.ndim - 1 - dim))

    near = jax.random.permutation(rng, blocks)[block_of(target)]
    far = (block_of(target) + blocks // 2) % blocks
    return jnp.where((block_of(source) == near) | (block_of(source) == far), factor * drawn, drawn)


def steps_of(rng, shape, shards, smallest, top_value):
    level, own = 1.0, jax.random.fold_in(rng, 6)
    for axis_at, parts in shards:
        draws = jnp.exp(jax.random.uniform(jax.random.fold_in(own, axis_at), (parts,), jnp.float32, smallest / len(shards), top_value / len(shards)))
        level = level * jnp.repeat(draws, shape[axis_at] // parts).reshape([-1 if axis == axis_at else 1 for axis in range(len(shape))])
    return level


def scatter_about(key, extent, scale, reach, shards=(), held_as=jnp.bfloat16):
    level = steps_of(key, extent, shards, -0.22, 0.18) if shards else 1.0
    values = jax.random.normal(key, extent, jnp.float32) * scale * level
    return jnp.minimum(jnp.maximum(values, -reach), reach).astype(held_as)


def heavy_noise(own_key, extent, spread, bound, pieces, heavy, held_as=jnp.bfloat16):
    entries = spread * jax.random.normal(own_key, extent, jnp.float32)
    if pieces:
        entries = entries * steps_of(own_key, extent, pieces, -0.22, 0.18)
    return jnp.clip(with_spikes(entries, jax.random.fold_in(own_key, 3), *heavy), -bound, bound).astype(held_as)


def setup_inputs(seed: int = 0) -> dict:
    seeds = jax.random.split(jax.random.key(seed), 7)
    voltages = heavy_noise(seeds[0], (2, ANTENNA_COUNT, CHANNEL_COUNT, TIME_SAMPLES), 1.0, 6.0, ((1, 16), (2, 8)), (1, 3, 16, 2.0))
    antenna_gains = scatter_about(seeds[1], (2, ANTENNA_COUNT, CHANNEL_COUNT), ANTENNA_COUNT ** -0.5, 0.75, ((2, 8),), jnp.float32)
    chirp_phase = jnp.clip(jax.random.uniform(seeds[2], (CHANNEL_COUNT, NFFT), jnp.float32, -3.140625, 3.140625), -3.140625, 3.140625)
    offsets = draw_offsets(jax.random.fold_in(seeds[6], 71), 0)
    flags = place_ends((jax.random.randint(seeds[4], (CHANNEL_COUNT, NWIN), 0, 8) < 1).astype(jnp.int32), jax.random.fold_in(seeds[4], 1), 0, 1)
    sample_phase_bins = place_ends(jax.random.randint(seeds[5], (TIME_SAMPLES,), 0, BINS), jax.random.fold_in(seeds[5], 1), 0, BINS - 1).astype(jnp.int32)
    return {"voltages": voltages, "antenna_gains": antenna_gains, "chirp_phase": chirp_phase, "offsets": offsets, "flags": flags, "sample_phase_bins": sample_phase_bins}


SK_WIDTH = 0.05
EPSILON = 1e-6


def reference(voltages, antenna_gains, chirp_phase, offsets, flags, sample_phase_bins):
    def beam_channel(channel):
        samples = lax.dynamic_index_in_dim(voltages, channel, 2, keepdims=False).astype(jnp.float32)
        weights = lax.dynamic_index_in_dim(antenna_gains, channel, 2, keepdims=False)
        weight_real = weights[0][:, None]
        weight_imag = weights[1][:, None]
        out_real = jnp.sum(weight_real * samples[0] - weight_imag * samples[1], axis=0)
        out_imag = jnp.sum(weight_real * samples[1] + weight_imag * samples[0], axis=0)
        return jnp.stack([out_real, out_imag])

    beam_sum = lax.map(beam_channel, jnp.arange(CHANNEL_COUNT, dtype=jnp.int32))

    def dedisperse_channel(items):
        beam_pair, phase_row, start_at = items
        padded = jnp.pad(beam_pair, ((0, 0), (TS, TS)))
        shifted = lax.dynamic_slice_in_dim(padded, start_at.astype(jnp.int32), TIME_SAMPLES + TS, 1)
        blocks = shifted.reshape(2, N_TM + 1, TS)
        segments = jnp.concatenate([blocks[:, :-1], blocks[:, 1:]], axis=2)
        signal = lax.complex(segments[0], segments[1])
        response = lax.complex(jnp.cos(phase_row), jnp.sin(phase_row))
        spectrum = jnp.fft.fft(signal, axis=-1) * response[None, :]
        result = jnp.fft.ifft(spectrum, axis=-1)[:, TS:].reshape(TIME_SAMPLES)
        return jnp.stack([jnp.real(result), jnp.imag(result)])

    output_pair = lax.map(dedisperse_channel, (beam_sum, chirp_phase, offsets))
    output_pair = jnp.moveaxis(output_pair, 1, 0)
    dedispersed = output_pair.astype(jnp.bfloat16)
    power = output_pair[0] * output_pair[0] + output_pair[1] * output_pair[1]
    windows = power.reshape(CHANNEL_COUNT, NWIN, SKW)
    first_sum = jnp.sum(windows, axis=-1)
    second_sum = jnp.sum(windows * windows, axis=-1)
    kurtosis = (SKW + 1.0) / (SKW - 1.0) * (SKW * second_sum / (first_sum * first_sum + EPSILON) - 1.0)
    keep = (1 - flags).astype(jnp.float32)
    sk_weight = keep / (1.0 + ((kurtosis - 1.0) / SK_WIDTH) ** 2)
    weighted = (sk_weight[:, :, None] * windows).reshape(CHANNEL_COUNT, TIME_SAMPLES).astype(jnp.bfloat16)

    def fold_channel(row_values):
        return jax.ops.segment_sum(row_values.astype(jnp.float32), sample_phase_bins, BINS)

    profile = jax.vmap(fold_channel)(weighted) * (BINS / TIME_SAMPLES)
    band_profile = jnp.sum(profile, axis=0)
    return dedispersed, sk_weight, profile, band_profile
```

```python
import math

import jax
import jax.numpy as jnp
import ml_dtypes
import numpy as np
from jax import lax
from jax.experimental import pallas as pl
from jax.experimental.pallas import tpu as pltpu
from jax.sharding import PartitionSpec as P

NFFT = 131072
HALF = NFFT // 2
SIDE = 256
OFFSET_BOUND = 4096
SKW = 1024
BINS = 2048
SK_WIDTH = 0.05
EPSILON = 1e-06
GRID_SIDE = 4
N_TM = 16
LANES = 128
BEAM_SCALE = 64.0

F32 = jnp.float32
BF16 = jnp.bfloat16
WIRE = jnp.float16


def split_table(table):
    high = table.astype(np.float32).astype(ml_dtypes.bfloat16)
    low = (table - high.astype(np.float64)).astype(np.float32).astype(ml_dtypes.bfloat16)
    return np.stack([high, low])


def circle(turns, length):
    angle = 2.0 * math.pi / length * (turns % length)
    return np.cos(angle), np.sin(angle)


def make_tables():
    index = np.arange(SIDE, dtype=np.int64)
    even = circle(index[:, None] * index[None, :], SIDE)
    odd = circle((2 * index[:, None] + 1) * index[None, :], 2 * SIDE)
    odd_back = (odd[0].T, odd[1].T)
    left_even = split_table(np.concatenate(even, axis=1))
    left_odd = split_table(np.concatenate(odd, axis=1))
    left_back = split_table(np.concatenate(odd_back, axis=1))
    right = split_table(np.concatenate(even, axis=0))
    twist = []
    for parity in (0, 1):
        row = 2 * index[:, None] + parity
        twist.append(np.stack(circle(row * index[None, :], NFFT)))
    twist = np.stack(twist).astype(np.float32)
    group = (index[:, None] // 4 == index[None, :] // 4).astype(np.float32)
    return left_even, left_odd, left_back, right, twist, group


def steps(down, across):
    side = GRID_SIDE
    return [
        (s, (s // side + down) % side * side + (s % side + across) % side)
        for s in range(side * side)
    ]


def beam_body(blocks, gains, samples, out, table):
    @pl.when(pl.program_id(0) == 0)
    def build():
        shape = (128, 256)
        row = lax.broadcasted_iota(jnp.int32, shape, 0)
        col = lax.broadcasted_iota(jnp.int32, shape, 1)
        part = row // 64
        imag_out = row // 32 % 2
        slot = row % 32
        chunk = jnp.where(slot < 16, 2 * slot, 2 * (slot - 16) + 1)
        from_imag = col // 128
        source = col % 128 // 4
        antenna = col % 4
        real = jnp.zeros(shape, F32)
        imag = jnp.zeros(shape, F32)
        for a in range(4):
            real = jnp.where(antenna == a, gains[0, a], real)
            imag = jnp.where(antenna == a, gains[1, a], imag)
        cross = jnp.where(imag_out == 1, imag, -imag)
        value = jnp.where(imag_out == from_imag, real, cross) * BEAM_SCALE
        value = jnp.where(chunk == source, value, 0.0)
        high = value.astype(BF16).astype(F32)
        table[...] = jnp.where(part == 0, high, value - high).astype(BF16)

    weights = table[...]
    for pair in range(4):
        columns = []
        for group in (2 * pair, 2 * pair + 1):
            rows = pl.ds(group * 128, 128)
            columns.append(jnp.concatenate([samples[0, rows, :], samples[1, rows, :]], axis=0))
        product = jnp.dot(
            weights, jnp.concatenate(columns, axis=1), preferred_element_type=F32
        )
        both = product[:64] + product[64:]
        for which in (0, 1):
            group = 2 * pair + which
            lanes = slice(which * 128, which * 128 + 128)
            rows = pl.ds(group * 16, 16)
            for comp in (0, 1):
                base = comp * 32
                out[0, comp, rows, 0:128] = both[base : base + 16, lanes]
                out[0, comp, rows, 128:256] = both[base + 16 : base + 32, lanes]


def beamform(blocks, gains, samples):
    grid_spec = pltpu.PrefetchScalarGridSpec(
        num_scalar_prefetch=1,
        grid=(4,),
        in_specs=[
            pl.BlockSpec(memory_space=pltpu.SMEM),
            pl.BlockSpec((2, 1024, LANES), lambda i, blocks: (0, blocks[i], 0)),
        ],
        out_specs=pl.BlockSpec((1, 2, 128, SIDE), lambda i, blocks: (i, 0, 0, 0)),
        scratch_shapes=[pltpu.VMEM((128, 256), BF16)],
    )
    return pl.pallas_call(
        beam_body,
        grid_spec=grid_spec,
        out_shape=jax.ShapeDtypeStruct((4, 2, 128, SIDE), F32),
        name="beamform",
    )(blocks, gains, samples)


def response_body(offset, phase, out):
    row = lax.broadcasted_iota(jnp.int32, (SIDE, SIDE), 0)
    col = lax.broadcasted_iota(jnp.int32, (SIDE, SIDE), 1)
    for parity in (0, 1):
        bin_index = 2 * row + parity + 512 * col
        turns = jnp.bitwise_and(bin_index * offset[0], NFFT - 1)
        turns = jnp.where(turns >= HALF, turns - NFFT, turns)
        angle = phase[parity] + turns.astype(F32) * (2.0 * math.pi / NFFT)
        out[parity, 0] = jnp.cos(angle)
        out[parity, 1] = jnp.sin(angle)


def make_response(offset, phase):
    return pl.pallas_call(
        response_body,
        in_specs=[pl.BlockSpec(memory_space=pltpu.SMEM), pl.BlockSpec(memory_space=pltpu.VMEM)],
        out_shape=jax.ShapeDtypeStruct((2, 2, SIDE, SIDE), F32),
        name="response",
    )(offset, phase)


def halves(value):
    high = value.astype(BF16)
    return high, (value - high.astype(F32)).astype(BF16)


def from_left(table, real, imag, sign):
    crossed = (imag, -real) if sign > 0 else (-imag, real)
    top = jnp.concatenate([real, imag], axis=1)
    bottom = jnp.concatenate(crossed, axis=1)
    high, low = halves(jnp.concatenate([top, bottom], axis=0))
    first, second = table[0], table[1]
    product = (
        jnp.dot(first, high, preferred_element_type=F32)
        + jnp.dot(first, low, preferred_element_type=F32)
        + jnp.dot(second, high, preferred_element_type=F32)
    )
    return product[:, :SIDE], product[:, SIDE:]


def from_right(real, imag, table, sign):
    crossed = (imag, -real) if sign > 0 else (-imag, real)
    left = jnp.concatenate([real, imag], axis=0)
    right = jnp.concatenate(crossed, axis=0)
    high, low = halves(jnp.concatenate([left, right], axis=1))
    first, second = table[0], table[1]
    product = (
        jnp.dot(high, first, preferred_element_type=F32)
        + jnp.dot(low, first, preferred_element_type=F32)
        + jnp.dot(high, second, preferred_element_type=F32)
    )
    return product[:SIDE], product[SIDE:]


def times(real, imag, other_real, other_imag):
    return real * other_real - imag * other_imag, real * other_imag + imag * other_real


def main_body(
    offset,
    own_ref,
    before_ref,
    after_ref,
    response,
    keep_ref,
    bins_ref,
    left_even,
    left_odd,
    left_back,
    right,
    twist,
    group,
    out_ref,
    weight_ref,
    profile_ref,
    high_ref,
    low_ref,
    value_ref,
):
    own = [own_ref[0], own_ref[1]]
    row = lax.broadcasted_iota(jnp.int32, (16, SIDE), 0)
    col = lax.broadcasted_iota(jnp.int32, (16, SIDE), 1)
    wrapped = row * SIDE + col < offset[0]
    before = []
    for comp in (0, 1):
        head = jnp.where(wrapped, after_ref[comp], before_ref[comp, 0:16, :])
        before.append(jnp.concatenate([head, before_ref[comp, 16:, :]], axis=0))
    back = []
    for parity, table in ((0, left_even), (1, left_odd)):
        sign = 1.0 if parity == 0 else -1.0
        real, imag = from_left(
            table, before[0] + sign * own[0], before[1] + sign * own[1], 1
        )
        cos, sin = twist[parity, 0], twist[parity, 1]
        real, imag = times(real, imag, cos, -sin)
        real, imag = from_right(real, imag, right, 1)
        real, imag = times(real, imag, response[parity, 0], response[parity, 1])
        real, imag = from_right(real, imag, right, -1)
        real, imag = times(real, imag, cos, sin)
        back.append(from_left(left_even if parity == 0 else left_back, real, imag, -1))
    scale = 1.0 / (NFFT * BEAM_SCALE)
    real = (back[0][0] - back[1][0]) * scale
    imag = (back[0][1] - back[1][1]) * scale
    out_ref[0] = real.astype(BF16)
    out_ref[1] = imag.astype(BF16)

    power = real * real + imag * imag
    row_one = jnp.broadcast_to(jnp.sum(power, axis=1, keepdims=True), (SIDE, LANES))
    row_two = jnp.broadcast_to(jnp.sum(power * power, axis=1, keepdims=True), (SIDE, LANES))
    rows = jnp.concatenate([row_one, row_two], axis=1)
    sums = jnp.dot(
        group[...], rows, preferred_element_type=F32, precision=lax.Precision.HIGHEST
    )
    first_sum, second_sum = sums[:, :LANES], sums[:, LANES:]
    kurtosis = (
        (SKW + 1.0) / (SKW - 1.0) * (SKW * second_sum / (first_sum * first_sum + EPSILON) - 1.0)
    )
    weight = keep_ref[...] / (1.0 + ((kurtosis - 1.0) / SK_WIDTH) ** 2)
    weight_ref[...] = weight
    value_ref[...] = (
        jnp.concatenate([weight, weight], axis=1) * power
    ).astype(BF16).astype(F32)

    bins = bins_ref[...]
    high_ref[...] = (bins // LANES).astype(F32)
    low_ref[...] = (bins % LANES).astype(F32)

    per_step = 8
    high_rows = lax.broadcasted_iota(jnp.int32, (16, SIDE), 0).astype(F32).astype(BF16)
    low_rows = lax.broadcasted_iota(jnp.int32, (LANES, SIDE), 0).astype(F32).astype(BF16)
    one, zero = jnp.ones((), BF16), jnp.zeros((), BF16)

    def fold(step, total):
        start = pl.multiple_of(step * per_step, per_step)
        high_block = high_ref[pl.ds(start, per_step), :]
        low_block = low_ref[pl.ds(start, per_step), :]
        value_block = value_ref[pl.ds(start, per_step), :]
        spreads, marks = [], []
        for r in range(per_step):
            high = jnp.broadcast_to(high_block[r : r + 1], (16, SIDE)).astype(BF16)
            value = jnp.broadcast_to(value_block[r : r + 1], (16, SIDE)).astype(BF16)
            spreads.append(jnp.where(high == high_rows, value, zero))
            low = jnp.broadcast_to(low_block[r : r + 1], (LANES, SIDE)).astype(BF16)
            marks.append(jnp.where(low == low_rows, one, zero))
        return total + lax.dot_general(
            jnp.concatenate(spreads, axis=1),
            jnp.concatenate(marks, axis=1),
            (((1,), (1,)), ((), ())),
            preferred_element_type=F32,
        )

    total = lax.fori_loop(0, SIDE // per_step, fold, jnp.zeros((16, LANES), F32))
    profile_ref[...] = total * (BINS / (HALF * N_TM))


def filter_and_fold(offset, own, before, after, response, keep, bins, tables):
    vmem = pl.BlockSpec(memory_space=pltpu.VMEM)
    return pl.pallas_call(
        main_body,
        in_specs=[pl.BlockSpec(memory_space=pltpu.SMEM)] + [vmem] * (6 + len(tables)),
        out_shape=(
            jax.ShapeDtypeStruct((2, SIDE, SIDE), BF16),
            jax.ShapeDtypeStruct((SIDE, LANES), F32),
            jax.ShapeDtypeStruct((16, LANES), F32),
        ),
        scratch_shapes=[pltpu.VMEM((SIDE, SIDE), F32)] * 3,
        compiler_params=pltpu.CompilerParams(vmem_limit_bytes=48 * 1024 * 1024),
        name="filter_and_fold",
    )(offset, own, before, after, response, keep, bins, *tables)


def send(value, down, across):
    return lax.ppermute(value, "tm", steps(down, across))


def sum_of(parts):
    total = parts[0].astype(F32)
    for part in parts[1:]:
        total = total + part.astype(F32)
    return total


def on_device(voltages, antenna_gains, chirp_phase, offsets, flags, sample_phase_bins):
    tables = make_tables()
    my_index = lax.axis_index("tm")
    down_at, across_at = my_index // GRID_SIDE, my_index % GRID_SIDE
    samples = (
        voltages.reshape(2, 4, TIME_CHUNKS, LANES)
        .transpose(0, 2, 1, 3)
        .reshape(2, TIME_CHUNKS * 4, LANES)
    )
    gains = lax.dynamic_slice_in_dim(antenna_gains[:, :, 0], my_index * 4, 4, 1)
    around = jnp.arange(GRID_SIDE, dtype=jnp.int32)

    order = (2, 1, 3, 0)
    partial = []
    for half in (0, 1):
        got = []
        for first in order:
            if half == 0:
                rows, cols = (down_at + first) % GRID_SIDE, (across_at + around) % GRID_SIDE
            else:
                rows, cols = (down_at + around) % GRID_SIDE, (across_at + first) % GRID_SIDE
            blocks = ((rows * GRID_SIDE + cols) * 2 + half).astype(jnp.int32)
            message = beamform(blocks, gains, samples)
            if first:
                wire = message.astype(WIRE)
                message = send(wire, first, 0) if half == 0 else send(wire, 0, first)
            got.append(message)
        partial.append(got)
    beam = []
    for half in (0, 1):
        got = []
        for second in order:
            part = sum_of([message[second] for message in partial[half]])
            if second:
                wire = part.astype(WIRE)
                part = send(wire, 0, second) if half == 0 else send(wire, second, 0)
            got.append(part)
        beam.append(sum_of(got))
    shards = N_TM
    ahead = [(s, s + 1) for s in range(shards - 1)]
    behind = [(s + 1, s) for s in range(shards - 1)]
    before = [lax.ppermute(part.astype(WIRE), "tm", ahead) for part in beam]
    after = lax.ppermute(beam[0][:, :16].astype(WIRE), "tm", behind)
    own = jnp.concatenate(beam, axis=1)
    before = jnp.concatenate(before, axis=1).astype(F32)
    after = after.astype(F32)

    phase = jnp.transpose(chirp_phase.reshape(SIDE, 2 * SIDE), (1, 0))
    phase = phase.reshape(SIDE, 2, SIDE).transpose(1, 0, 2)
    response = make_response(offsets, phase)
    keep = jnp.broadcast_to((1 - flags).astype(F32).reshape(64, 1, 1), (64, 4, LANES))
    keep = keep.reshape(SIDE, LANES)
    bins = sample_phase_bins.reshape(SIDE, SIDE)
    filtered, weight, partial_profile = filter_and_fold(
        offsets, own, before, after, response, keep, bins, tables
    )
    dedispersed = filtered.reshape(2, 1, HALF)
    sk_weight = weight.reshape(64, 4, LANES)[:, 0, 0].reshape(1, 64)
    channels = lax.axis_size("chan")
    pieces = jnp.broadcast_to(partial_profile[None], (channels, N_TM, LANES))
    arrived = lax.all_to_all(
        pieces.reshape(channels * N_TM, LANES), ("chan", "tm"), 0, 0, tiled=True
    ).reshape(channels, N_TM, LANES)
    by_channel = jnp.sum(arrived, axis=1)
    profile = lax.dynamic_slice_in_dim(by_channel, lax.axis_index("chan"), 1, 0)
    band_profile = jnp.sum(by_channel, axis=0)
    return (dedispersed, sk_weight, profile, band_profile)


TIME_CHUNKS = 1048576 // LANES


def solution(mesh):
    placed = (
        P(None, "tm", "chan", None),
        P(None, None, "chan"),
        P("chan", None),
        P("chan"),
        P("chan", "tm"),
        P("tm"),
    )
    return jax.shard_map(
        on_device,
        mesh=mesh,
        in_specs=placed,
        out_specs=(P(None, "chan", "tm"), P("chan", "tm"), P("chan", "tm"), P("tm")),
        check_vma=False,
    )
```

```python
import math

import jax
import jax.numpy as jnp
import ml_dtypes
import numpy as np
from jax import lax
from jax.experimental import pallas as pl
from jax.experimental.pallas import tpu as pltpu
from jax.sharding import PartitionSpec as P

NFFT = 131072
HALF = NFFT // 2
SIDE = 256
OFFSET_BOUND = 4096
SKW = 1024
BINS = 2048
SK_WIDTH = 0.05
EPSILON = 1e-06
GRID_SIDE = 4
N_TM = 16
LANES = 128

F32 = jnp.float32
BF16 = jnp.bfloat16


def split_table(table):
    high = table.astype(np.float32).astype(ml_dtypes.bfloat16)
    low = (table - high.astype(np.float64)).astype(np.float32).astype(ml_dtypes.bfloat16)
    return np.stack([high, low])


def circle(turns, length):
    angle = 2.0 * math.pi / length * (turns % length)
    return np.cos(angle), np.sin(angle)


def make_tables():
    index = np.arange(SIDE, dtype=np.int64)
    even = circle(index[:, None] * index[None, :], SIDE)
    odd = circle((2 * index[:, None] + 1) * index[None, :], 2 * SIDE)
    odd_back = (odd[0].T, odd[1].T)
    left_even = split_table(np.concatenate(even, axis=1))
    left_odd = split_table(np.concatenate(odd, axis=1))
    left_back = split_table(np.concatenate(odd_back, axis=1))
    right = split_table(np.concatenate(even, axis=0))
    twist = []
    for parity in (0, 1):
        row = 2 * index[:, None] + parity
        twist.append(np.stack(circle(row * index[None, :], NFFT)))
    twist = np.stack(twist).astype(np.float32)
    group = (index[:, None] // 4 == index[None, :] // 4).astype(np.float32)
    return left_even, left_odd, left_back, right, twist, group


def steps(down, across):
    side = GRID_SIDE
    return [
        (s, (s // side + down) % side * side + (s % side + across) % side)
        for s in range(side * side)
    ]


CODE_TOP = 32000.0
HEADER = 16
ROWS = 2 * 128 + HEADER


def encode(real, imag):
    top = jnp.maximum(jnp.max(jnp.abs(real), axis=0, keepdims=True), jnp.max(jnp.abs(imag), axis=0, keepdims=True))
    top = jnp.broadcast_to(jnp.max(top, axis=1, keepdims=True), (8, SIDE))
    level = jnp.floor(4.0 * jnp.log2(CODE_TOP / jnp.maximum(top, 1e-30)))
    scale = jnp.exp2(0.25 * level)[0:1]
    whole = lambda value: jnp.round(value).astype(jnp.int32).astype(jnp.int16)
    header = jnp.concatenate([level, level], axis=0)
    return whole(real * scale), whole(imag * scale), whole(header)


def decode(block_ref, *lead):
    level = block_ref[(*lead, pl.ds(2 * 128, HEADER), slice(None))].astype(jnp.int32).astype(F32)
    step = jnp.exp2(-0.25 * level)[0:1]
    parts = []
    for comp in (0, 1):
        code = block_ref[(*lead, pl.ds(comp * 128, 128), slice(None))]
        parts.append(code.astype(jnp.int32).astype(F32) * step)
    return parts


def beam_body(messages, index, gains, samples, *refs):
    outs = refs[: len(messages)]
    table, buffer, arrived = refs[len(messages) :]
    down_at = index[0] // GRID_SIDE
    across_at = index[0] % GRID_SIDE

    def copy_of(slot, half, step, j):
        if half == 0:
            rows, cols = down_at + step, across_at + j
        else:
            rows, cols = down_at + j, across_at + step
        block = (rows % GRID_SIDE * GRID_SIDE + cols % GRID_SIDE) * 2 + half
        first = pl.multiple_of(block * 1024, 1024)
        return pltpu.make_async_copy(
            samples.at[:, pl.ds(first, 1024), :], buffer.at[slot], arrived.at[slot]
        )

    copies = []
    for number, (half, step) in enumerate(messages):
        copies.append([copy_of(number * 4 + j, half, step, j) for j in range(4)])
        for copy in copies[-1]:
            copy.start()

    shape = (128, 256)
    row = lax.broadcasted_iota(jnp.int32, shape, 0)
    col = lax.broadcasted_iota(jnp.int32, shape, 1)
    part = row // 64
    imag_out = row // 32 % 2
    slot = row % 32
    chunk = jnp.where(slot < 16, 2 * slot, 2 * (slot - 16) + 1)
    from_imag = col // 128
    source = col % 128 // 4
    antenna = col % 4
    real = jnp.zeros(shape, F32)
    imag = jnp.zeros(shape, F32)
    for a in range(4):
        real = jnp.where(antenna == a, gains[0, 0, index[0] * 4 + a], real)
        imag = jnp.where(antenna == a, gains[1, 0, index[0] * 4 + a], imag)
    cross = jnp.where(imag_out == 1, imag, -imag)
    value = jnp.where(imag_out == from_imag, real, cross)
    value = jnp.where(chunk == source, value, 0.0)
    high = value.astype(BF16).astype(F32)
    table[...] = jnp.where(part == 0, high, value - high).astype(BF16)

    for number in range(len(messages)):
        for j in range(4):
            copies[number][j].wait()
            weights = table[...]
            at = number * 4 + j
            columns = []
            for group in range(8):
                rows = pl.ds(group * 128, 128)
                columns.append(
                    jnp.concatenate([buffer[at, 0, rows, :], buffer[at, 1, rows, :]], axis=0)
                )
            product = jnp.dot(
                weights, jnp.concatenate(columns, axis=1), preferred_element_type=F32
            )
            both = product[:64] + product[64:]
            planes = []
            for comp in (0, 1):
                lanes = lambda base: jnp.concatenate(
                    [both[base : base + 16, g * 128 : g * 128 + 128] for g in range(8)], axis=0
                )
                planes.append(
                    jnp.concatenate([lanes(comp * 32), lanes(comp * 32 + 16)], axis=1)
                )
            out = outs[number]
            out[j, 0:128], out[j, 128:256], out[j, 256:272] = encode(*planes)


def beamform(index, gains, samples, messages):
    count = len(messages)
    return pl.pallas_call(
        lambda *refs: beam_body(messages, *refs),
        in_specs=[
            pl.BlockSpec(memory_space=pltpu.SMEM),
            pl.BlockSpec(memory_space=pltpu.SMEM),
            pl.BlockSpec(memory_space=pl.ANY),
        ],
        out_shape=tuple(jax.ShapeDtypeStruct((4, ROWS, SIDE), jnp.int16) for _ in messages),
        scratch_shapes=[
            pltpu.VMEM((128, 256), BF16),
            pltpu.VMEM((count * 4, 2, 1024, LANES), BF16),
            pltpu.SemaphoreType.DMA((count * 4,)),
        ],
        compiler_params=pltpu.CompilerParams(vmem_limit_bytes=(count * 2 + 16) * 1024 * 1024),
        name="beamform",
    )(index, gains, samples)


def middle_body(order, *refs):
    parts, outs = refs[:4], refs[4:]
    for second, out in zip(order, outs):
        total = decode(parts[0], second)
        for part in parts[1:]:
            more = decode(part, second)
            total = [total[0] + more[0], total[1] + more[1]]
        if second:
            out[0:128], out[128:256], out[256:272] = encode(*total)
        else:
            out[0], out[1] = total


def middle(parts, order):
    return pl.pallas_call(
        lambda *refs: middle_body(order, *refs),
        out_shape=tuple(
            jax.ShapeDtypeStruct((ROWS, SIDE), jnp.int16)
            if second
            else jax.ShapeDtypeStruct((2, 128, SIDE), F32)
            for second in order
        ),
        compiler_params=pltpu.CompilerParams(vmem_limit_bytes=16 * 1024 * 1024),
        name="middle",
    )(*parts)


def last_body(*refs):
    parts, (own, ahead, behind) = refs[:8], refs[8:]
    for half in (0, 1):
        mine = parts[half * 4]
        total = [mine[0], mine[1]]
        for part in parts[half * 4 + 1 : half * 4 + 4]:
            more = decode(part)
            total = [total[0] + more[0], total[1] + more[1]]
        rows = pl.ds(half * 128, 128)
        own[0, rows], own[1, rows] = total
        ahead[half, 0:128], ahead[half, 128:256], ahead[half, 256:272] = encode(*total)
        if half == 0:
            behind[0], behind[1] = total[0][0:16], total[1][0:16]


def last(parts):
    return pl.pallas_call(
        last_body,
        out_shape=(
            jax.ShapeDtypeStruct((2, SIDE, SIDE), F32),
            jax.ShapeDtypeStruct((2, ROWS, SIDE), jnp.int16),
            jax.ShapeDtypeStruct((2, 16, SIDE), F32),
        ),
        compiler_params=pltpu.CompilerParams(vmem_limit_bytes=16 * 1024 * 1024),
        name="last",
    )(*parts)


def response_body(offset, phase, out):
    row = lax.broadcasted_iota(jnp.int32, (SIDE, SIDE), 0)
    col = lax.broadcasted_iota(jnp.int32, (SIDE, SIDE), 1)
    for parity in (0, 1):
        bin_index = 2 * row + parity + 512 * col
        turns = jnp.bitwise_and(bin_index * offset[0], NFFT - 1)
        turns = jnp.where(turns >= HALF, turns - NFFT, turns)
        angle = phase[parity] + turns.astype(F32) * (2.0 * math.pi / NFFT)
        out[parity, 0] = jnp.cos(angle)
        out[parity, 1] = jnp.sin(angle)


def make_response(offset, phase):
    return pl.pallas_call(
        response_body,
        in_specs=[pl.BlockSpec(memory_space=pltpu.SMEM), pl.BlockSpec(memory_space=pltpu.VMEM)],
        out_shape=jax.ShapeDtypeStruct((2, 2, SIDE, SIDE), F32),
        name="response",
    )(offset, phase)


def halves(value):
    high = value.astype(BF16)
    return high, (value - high.astype(F32)).astype(BF16)


def from_left(table, real, imag, sign):
    crossed = (imag, -real) if sign > 0 else (-imag, real)
    top = jnp.concatenate([real, imag], axis=1)
    bottom = jnp.concatenate(crossed, axis=1)
    high, low = halves(jnp.concatenate([top, bottom], axis=0))
    first, second = table[0], table[1]
    product = (
        jnp.dot(first, high, preferred_element_type=F32)
        + jnp.dot(first, low, preferred_element_type=F32)
        + jnp.dot(second, high, preferred_element_type=F32)
    )
    return product[:, :SIDE], product[:, SIDE:]


def from_right(real, imag, table, sign):
    crossed = (imag, -real) if sign > 0 else (-imag, real)
    left = jnp.concatenate([real, imag], axis=0)
    right = jnp.concatenate(crossed, axis=0)
    high, low = halves(jnp.concatenate([left, right], axis=1))
    first, second = table[0], table[1]
    product = (
        jnp.dot(high, first, preferred_element_type=F32)
        + jnp.dot(low, first, preferred_element_type=F32)
        + jnp.dot(high, second, preferred_element_type=F32)
    )
    return product[:SIDE], product[SIDE:]


def times(real, imag, other_real, other_imag):
    return real * other_real - imag * other_imag, real * other_imag + imag * other_real


def main_body(
    offset,
    own_ref,
    before_ref,
    after_ref,
    response,
    keep_ref,
    bins_ref,
    left_even,
    left_odd,
    left_back,
    right,
    twist,
    group,
    out_ref,
    weight_ref,
    profile_ref,
    high_ref,
    low_ref,
    value_ref,
):
    own = [own_ref[0], own_ref[1]]
    row = lax.broadcasted_iota(jnp.int32, (16, SIDE), 0)
    col = lax.broadcasted_iota(jnp.int32, (16, SIDE), 1)
    wrapped = row * SIDE + col < offset[0]
    earlier = [decode(before_ref, 0), decode(before_ref, 1)]
    before = []
    for comp in (0, 1):
        head = jnp.where(wrapped, after_ref[comp], earlier[0][comp][0:16])
        before.append(jnp.concatenate([head, earlier[0][comp][16:], earlier[1][comp]], axis=0))
    back = []
    for parity, table in ((0, left_even), (1, left_odd)):
        sign = 1.0 if parity == 0 else -1.0
        real, imag = from_left(
            table, before[0] + sign * own[0], before[1] + sign * own[1], 1
        )
        cos, sin = twist[parity, 0], twist[parity, 1]
        real, imag = times(real, imag, cos, -sin)
        real, imag = from_right(real, imag, right, 1)
        real, imag = times(real, imag, response[parity, 0], response[parity, 1])
        real, imag = from_right(real, imag, right, -1)
        real, imag = times(real, imag, cos, sin)
        back.append(from_left(left_even if parity == 0 else left_back, real, imag, -1))
    scale = 1.0 / NFFT
    real = (back[0][0] - back[1][0]) * scale
    imag = (back[0][1] - back[1][1]) * scale
    out_ref[0] = real.astype(BF16)
    out_ref[1] = imag.astype(BF16)

    power = real * real + imag * imag
    row_one = jnp.broadcast_to(jnp.sum(power, axis=1, keepdims=True), (SIDE, LANES))
    row_two = jnp.broadcast_to(jnp.sum(power * power, axis=1, keepdims=True), (SIDE, LANES))
    rows = jnp.concatenate([row_one, row_two], axis=1)
    sums = jnp.dot(
        group[...], rows, preferred_element_type=F32, precision=lax.Precision.HIGHEST
    )
    first_sum, second_sum = sums[:, :LANES], sums[:, LANES:]
    kurtosis = (
        (SKW + 1.0) / (SKW - 1.0) * (SKW * second_sum / (first_sum * first_sum + EPSILON) - 1.0)
    )
    weight = keep_ref[...] / (1.0 + ((kurtosis - 1.0) / SK_WIDTH) ** 2)
    weight_ref[...] = weight
    value_ref[...] = (
        jnp.concatenate([weight, weight], axis=1) * power
    ).astype(BF16).astype(F32)

    bins = bins_ref[...]
    high_ref[...] = (bins // LANES).astype(F32)
    low_ref[...] = (bins % LANES).astype(F32)

    per_step = 8
    high_rows = lax.broadcasted_iota(jnp.int32, (16, SIDE), 0).astype(F32).astype(BF16)
    low_rows = lax.broadcasted_iota(jnp.int32, (LANES, SIDE), 0).astype(F32).astype(BF16)
    one, zero = jnp.ones((), BF16), jnp.zeros((), BF16)

    def fold(step, total):
        start = pl.multiple_of(step * per_step, per_step)
        high_block = high_ref[pl.ds(start, per_step), :]
        low_block = low_ref[pl.ds(start, per_step), :]
        value_block = value_ref[pl.ds(start, per_step), :]
        spreads, marks = [], []
        for r in range(per_step):
            high = jnp.broadcast_to(high_block[r : r + 1], (16, SIDE)).astype(BF16)
            value = jnp.broadcast_to(value_block[r : r + 1], (16, SIDE)).astype(BF16)
            spreads.append(jnp.where(high == high_rows, value, zero))
            low = jnp.broadcast_to(low_block[r : r + 1], (LANES, SIDE)).astype(BF16)
            marks.append(jnp.where(low == low_rows, one, zero))
        return total + lax.dot_general(
            jnp.concatenate(spreads, axis=1),
            jnp.concatenate(marks, axis=1),
            (((1,), (1,)), ((), ())),
            preferred_element_type=F32,
        )

    total = lax.fori_loop(0, SIDE // per_step, fold, jnp.zeros((16, LANES), F32))
    profile_ref[...] = total * (BINS / (HALF * N_TM))


def filter_and_fold(offset, own, before, after, response, keep, bins, tables):
    vmem = pl.BlockSpec(memory_space=pltpu.VMEM)
    return pl.pallas_call(
        main_body,
        in_specs=[pl.BlockSpec(memory_space=pltpu.SMEM)] + [vmem] * (6 + len(tables)),
        out_shape=(
            jax.ShapeDtypeStruct((2, SIDE, SIDE), BF16),
            jax.ShapeDtypeStruct((SIDE, LANES), F32),
            jax.ShapeDtypeStruct((16, LANES), F32),
        ),
        scratch_shapes=[pltpu.VMEM((SIDE, SIDE), F32)] * 3,
        compiler_params=pltpu.CompilerParams(vmem_limit_bytes=48 * 1024 * 1024),
        name="filter_and_fold",
    )(offset, own, before, after, response, keep, bins, *tables)


def send(value, down, across):
    return lax.ppermute(value, "tm", steps(down, across))


def on_device(voltages, antenna_gains, chirp_phase, offsets, flags, sample_phase_bins):
    tables = make_tables()
    index = lax.axis_index("tm").astype(jnp.int32).reshape(1)
    samples = (
        voltages.reshape(2, 4, TIME_CHUNKS, LANES)
        .transpose(0, 2, 1, 3)
        .reshape(2, TIME_CHUNKS * 4, LANES)
    )
    gains = antenna_gains.transpose(0, 2, 1)
    order = (2, 1, 3, 0)

    def first_send(half, step, value):
        return send(value, step, 0) if half == 0 else send(value, 0, step)

    def second_send(half, step, value):
        return send(value, 0, step) if half == 0 else send(value, step, 0)

    got = [[], []]
    for messages in (((0, 2), (1, 2)), ((0, 1), (1, 1), (0, 3), (1, 3)), ((0, 0), (1, 0))):
        made = beamform(index, gains, samples, messages)
        for (half, step), value in zip(messages, made):
            got[half].append(first_send(half, step, value) if step else value)
    landed = [[], []]
    for half in (0, 1):
        made = middle(got[half], order)
        for step, value in zip(order, made):
            landed[half].append(second_send(half, step, value) if step else value)
    own, ahead, behind = last([landed[half][i] for half in (0, 1) for i in (3, 0, 1, 2)])
    before = lax.ppermute(ahead, "tm", [(s, s + 1) for s in range(N_TM - 1)])
    after = lax.ppermute(behind, "tm", [(s + 1, s) for s in range(N_TM - 1)])

    phase = jnp.transpose(chirp_phase.reshape(SIDE, 2 * SIDE), (1, 0))
    phase = phase.reshape(SIDE, 2, SIDE).transpose(1, 0, 2)
    response = make_response(offsets, phase)
    keep = jnp.broadcast_to((1 - flags).astype(F32).reshape(64, 1, 1), (64, 4, LANES))
    keep = keep.reshape(SIDE, LANES)
    bins = sample_phase_bins.reshape(SIDE, SIDE)
    filtered, weight, partial_profile = filter_and_fold(
        offsets, own, before, after, response, keep, bins, tables
    )
    dedispersed = filtered.reshape(2, 1, HALF)
    sk_weight = weight.reshape(64, 4, LANES)[:, 0, 0].reshape(1, 64)
    channels = lax.axis_size("chan")
    pieces = jnp.broadcast_to(partial_profile[None], (channels, N_TM, LANES))
    arrived = lax.all_to_all(
        pieces.reshape(channels * N_TM, LANES), ("chan", "tm"), 0, 0, tiled=True
    ).reshape(channels, N_TM, LANES)
    by_channel = jnp.sum(arrived, axis=1)
    profile = lax.dynamic_slice_in_dim(by_channel, lax.axis_index("chan"), 1, 0)
    band_profile = jnp.sum(by_channel, axis=0)
    return (dedispersed, sk_weight, profile, band_profile)


TIME_CHUNKS = 1048576 // LANES


def solution(mesh):
    placed = (
        P(None, "tm", "chan", None),
        P(None, None, "chan"),
        P("chan", None),
        P("chan"),
        P("chan", "tm"),
        P("tm"),
    )
    return jax.shard_map(
        on_device,
        mesh=mesh,
        in_specs=placed,
        out_specs=(P(None, "chan", "tm"), P("chan", "tm"), P("chan", "tm"), P("tm")),
        check_vma=False,
    )
```

```python
import math

import jax
import jax.numpy as jnp
import ml_dtypes
import numpy as np
from jax import lax
from jax.experimental import pallas as pl
from jax.experimental.pallas import tpu as pltpu
from jax.sharding import PartitionSpec as P

NFFT = 131072
HALF = NFFT // 2
SIDE = 256
OFFSET_BOUND = 4096
SKW = 1024
BINS = 2048
LOW_BINS = 64
HIGH_BINS = BINS // LOW_BINS
SK_WIDTH = 0.05
EPSILON = 1e-06
GRID_SIDE = 4
N_TM = 16
CHANNELS = 8
LANES = 128
QUARTER = 128

F32 = jnp.float32
BF16 = jnp.bfloat16


def split_table(table):
    high = table.astype(np.float32).astype(ml_dtypes.bfloat16)
    low = (table - high.astype(np.float64)).astype(np.float32).astype(ml_dtypes.bfloat16)
    return np.stack([high, low])


def circle(turns, length):
    angle = 2.0 * math.pi / length * (turns % length)
    return np.cos(angle), np.sin(angle)


def real_form(cos, sin):
    return split_table(np.block([[cos, sin], [-sin, cos]]))


def make_tables():
    index = np.arange(QUARTER, dtype=np.int64)
    rows_forward, rows_back, twist = [], [], []
    lanes = np.arange(SIDE, dtype=np.int64)
    for r in range(4):
        cos, sin = circle((4 * index[:, None] + r) * index[None, :], 2 * SIDE)
        rows_forward.append(real_form(cos, sin))
        rows_back.append(real_form(cos.T, -sin.T))
        twist.append(np.stack(circle((4 * index[:, None] + r) * lanes[None, :], NFFT)))
    columns_forward, columns_back = [], []
    for s in range(2):
        cos, sin = circle(index[:, None] * (2 * index[None, :] + s), SIDE)
        columns_forward.append(real_form(cos, -sin))
        columns_back.append(real_form(cos.T, sin.T))
    group = (lanes[:, None] // 4 == lanes[None, :] // 4).astype(np.float32)
    return (
        np.stack(rows_forward),
        np.stack(columns_forward),
        np.stack(columns_back),
        np.stack(rows_back),
        np.stack(twist).astype(np.float32),
        group,
    )


def steps(down, across):
    side = GRID_SIDE
    return [
        (s, (s // side + down) % side * side + (s % side + across) % side)
        for s in range(side * side)
    ]


CODE_TOP = 32000.0
HEADER = 16
ROWS = 2 * 128 + HEADER


def encode(real, imag):
    top = jnp.maximum(jnp.max(jnp.abs(real), axis=0, keepdims=True), jnp.max(jnp.abs(imag), axis=0, keepdims=True))
    top = jnp.broadcast_to(jnp.max(top, axis=1, keepdims=True), (8, SIDE))
    level = jnp.floor(4.0 * jnp.log2(CODE_TOP / jnp.maximum(top, 1e-30)))
    scale = jnp.exp2(0.25 * level)[0:1]
    whole = lambda value: jnp.round(value).astype(jnp.int32).astype(jnp.int16)
    header = jnp.concatenate([level, level], axis=0)
    return whole(real * scale), whole(imag * scale), whole(header)


def decode(block_ref, *lead):
    level = block_ref[(*lead, pl.ds(2 * 128, HEADER), slice(None))].astype(jnp.int32).astype(F32)
    step = jnp.exp2(-0.25 * level)[0:1]
    parts = []
    for comp in (0, 1):
        code = block_ref[(*lead, pl.ds(comp * 128, 128), slice(None))]
        parts.append(code.astype(jnp.int32).astype(F32) * step)
    return parts


def beam_body(messages, gains, samples, *refs):
    table, buffer, arrived = refs[-3:]
    outs = refs[-4 - len(messages) : -4]
    refs[-4][...] = jnp.zeros((8, LANES), F32)
    index = lax.axis_index("tm").astype(jnp.int32)
    down_at = index // GRID_SIDE
    across_at = index % GRID_SIDE

    def copy_of(slot, half, step, j):
        if half == 0:
            rows, cols = down_at + step, across_at + j
        else:
            rows, cols = down_at + j, across_at + step
        block = (rows % GRID_SIDE * GRID_SIDE + cols % GRID_SIDE) * 2 + half
        first = pl.multiple_of(block * 1024, 1024)
        return pltpu.make_async_copy(
            samples.at[:, pl.ds(first, 1024), :], buffer.at[slot], arrived.at[slot]
        )

    copies = []
    for number, (half, step) in enumerate(messages):
        copies.append([copy_of(number * 4 + j, half, step, j) for j in range(4)])
        for copy in copies[-1]:
            copy.start()

    shape = (128, 256)
    row = lax.broadcasted_iota(jnp.int32, shape, 0)
    col = lax.broadcasted_iota(jnp.int32, shape, 1)
    part = row // 64
    imag_out = row // 32 % 2
    slot = row % 32
    chunk = jnp.where(slot < 16, 2 * slot, 2 * (slot - 16) + 1)
    from_imag = col // 128
    source = col % 128 // 4
    antenna = col % 4
    antennas = lax.broadcasted_iota(jnp.int32, (1, 64), 1)
    real = jnp.zeros(shape, F32)
    imag = jnp.zeros(shape, F32)
    for a in range(4):
        own = antennas == index * 4 + a
        pick = lambda comp: jnp.sum(jnp.where(own, gains[comp], 0.0), axis=1, keepdims=True)
        real = jnp.where(antenna == a, pick(0), real)
        imag = jnp.where(antenna == a, pick(1), imag)
    cross = jnp.where(imag_out == 1, imag, -imag)
    value = jnp.where(imag_out == from_imag, real, cross)
    value = jnp.where(chunk == source, value, 0.0)
    high = value.astype(BF16).astype(F32)
    table[...] = jnp.where(part == 0, high, value - high).astype(BF16)

    for number in range(len(messages)):
        for j in range(4):
            copies[number][j].wait()
            weights = table[...]
            at = number * 4 + j
            columns = []
            for group in range(8):
                rows = pl.ds(group * 128, 128)
                columns.append(
                    jnp.concatenate([buffer[at, 0, rows, :], buffer[at, 1, rows, :]], axis=0)
                )
            product = jnp.dot(
                weights, jnp.concatenate(columns, axis=1), preferred_element_type=F32
            )
            both = product[:64] + product[64:]
            planes = []
            for comp in (0, 1):
                lanes = lambda base: jnp.concatenate(
                    [both[base : base + 16, g * 128 : g * 128 + 128] for g in range(8)], axis=0
                )
                planes.append(
                    jnp.concatenate([lanes(comp * 32), lanes(comp * 32 + 16)], axis=1)
                )
            out = outs[number]
            out[j, 0:128], out[j, 128:256], out[j, 256:272] = encode(*planes)


def beamform(gains, samples, messages, ready=()):
    count = len(messages)
    return pl.pallas_call(
        lambda *refs: beam_body(messages, *refs),
        in_specs=[
            pl.BlockSpec(memory_space=pltpu.VMEM),
            pl.BlockSpec(memory_space=pltpu.HBM),
        ]
        + [pl.BlockSpec(memory_space=pltpu.VMEM)] * len(ready),
        out_shape=tuple(jax.ShapeDtypeStruct((4, ROWS, SIDE), jnp.int16) for _ in messages)
        + (jax.ShapeDtypeStruct((8, LANES), F32),),
        scratch_shapes=[
            pltpu.VMEM((128, 256), BF16),
            pltpu.VMEM((count * 4, 2, 1024, LANES), BF16),
            pltpu.SemaphoreType.DMA((count * 4,)),
        ],
        compiler_params=pltpu.CompilerParams(vmem_limit_bytes=50 * 1024 * 1024),
        name="beamform",
    )(gains, samples, *ready)


def middle_body(order, *refs):
    parts, outs = refs[:4], refs[4:]
    for second, out in zip(order, outs):
        total = decode(parts[0], second)
        for part in parts[1:]:
            more = decode(part, second)
            total = [total[0] + more[0], total[1] + more[1]]
        if second:
            out[0:128], out[128:256], out[256:272] = encode(*total)
        else:
            out[0], out[1] = total


def middle(parts, order):
    return pl.pallas_call(
        lambda *refs: middle_body(order, *refs),
        out_shape=tuple(
            jax.ShapeDtypeStruct((ROWS, SIDE), jnp.int16)
            if second
            else jax.ShapeDtypeStruct((2, 128, SIDE), F32)
            for second in order
        ),
        compiler_params=pltpu.CompilerParams(vmem_limit_bytes=16 * 1024 * 1024),
        name="middle",
    )(*parts)


def last_body(*refs):
    parts, (own, ahead, behind) = refs[:8], refs[8:]
    for half in (0, 1):
        mine = parts[half * 4]
        total = [mine[0], mine[1]]
        for part in parts[half * 4 + 1 : half * 4 + 4]:
            more = decode(part)
            total = [total[0] + more[0], total[1] + more[1]]
        rows = pl.ds(half * 128, 128)
        own[0, rows], own[1, rows] = total
        ahead[half, 0:128], ahead[half, 128:256], ahead[half, 256:272] = encode(*total)
        if half == 0:
            behind[0], behind[1] = total[0][0:16], total[1][0:16]


def last(parts):
    return pl.pallas_call(
        last_body,
        out_shape=(
            jax.ShapeDtypeStruct((2, SIDE, SIDE), F32),
            jax.ShapeDtypeStruct((2, ROWS, SIDE), jnp.int16),
            jax.ShapeDtypeStruct((2, 16, SIDE), F32),
        ),
        compiler_params=pltpu.CompilerParams(vmem_limit_bytes=16 * 1024 * 1024),
        name="last",
    )(*parts)


def response_body(offset, phase, out, turned):
    row = lax.broadcasted_iota(jnp.int32, (QUARTER, LANES), 0)
    col = lax.broadcasted_iota(jnp.int32, (QUARTER, LANES), 1)
    for s in (0, 1):
        for part in range(4):
            block = phase[pl.ds(part + 4 * s, LANES, stride=8), :]
            turned[s, pl.ds(part * LANES, LANES), :] = jnp.transpose(block)
        for r in range(4):
            bin_index = 4 * row + r + 512 * (2 * col + s)
            turns = jnp.bitwise_and(bin_index * offset[0], NFFT - 1)
            turns = jnp.where(turns >= HALF, turns - NFFT, turns)
            angle = turned[s, pl.ds(r, QUARTER, stride=4), :]
            angle = angle + turns.astype(F32) * (2.0 * math.pi / NFFT)
            rows = pl.ds(r * QUARTER, QUARTER)
            out[s, 0, rows, :] = jnp.cos(angle)
            out[s, 1, rows, :] = jnp.sin(angle)


def make_response(offset, phase):
    return pl.pallas_call(
        response_body,
        in_specs=[pl.BlockSpec(memory_space=pltpu.SMEM), pl.BlockSpec(memory_space=pltpu.VMEM)],
        out_shape=jax.ShapeDtypeStruct((2, 2, 2 * SIDE, LANES), F32),
        scratch_shapes=[pltpu.VMEM((2, 2 * SIDE, LANES), F32)],
        compiler_params=pltpu.CompilerParams(vmem_limit_bytes=16 * 1024 * 1024),
        name="response",
    )(offset, phase)


def halves(value):
    high = value.astype(BF16)
    return high, (value - high.astype(F32)).astype(BF16)


def from_left(table, value):
    high, low = halves(value)
    first, second = table[0], table[1]
    return (
        jnp.dot(first, high, preferred_element_type=F32)
        + jnp.dot(first, low, preferred_element_type=F32)
        + jnp.dot(second, high, preferred_element_type=F32)
    )


def from_right(value, table):
    high, low = halves(value)
    first, second = table[0], table[1]
    return (
        jnp.dot(high, first, preferred_element_type=F32)
        + jnp.dot(low, first, preferred_element_type=F32)
        + jnp.dot(high, second, preferred_element_type=F32)
    )


def quarter_turn(pair, count):
    real, imag = pair
    return ((real, imag), (-imag, real), (-real, -imag), (imag, -real))[count % 4]


def add(first, second):
    return first[0] + second[0], first[1] + second[1]


def four_point(parts, sign):
    even = add(parts[0], parts[2]), add(parts[1], parts[3])
    odd = add(parts[0], quarter_turn(parts[2], 2)), add(parts[1], quarter_turn(parts[3], 2))
    return (
        add(even[0], even[1]),
        add(odd[0], quarter_turn(odd[1], sign)),
        add(even[0], quarter_turn(even[1], 2)),
        add(odd[0], quarter_turn(odd[1], -sign)),
    )


def times(real, imag, other_real, other_imag):
    return real * other_real - imag * other_imag, real * other_imag + imag * other_real


def main_body(
    offset,
    own_ref,
    before_ref,
    after_ref,
    response,
    flags_ref,
    bins_ref,
    rows_forward,
    columns_forward,
    columns_back,
    rows_back,
    twist,
    group,
    out_ref,
    weight_ref,
    profile_ref,
    high_ref,
    low_ref,
    value_ref,
    total_ref,
):
    own = [own_ref[0], own_ref[1]]
    row = lax.broadcasted_iota(jnp.int32, (16, SIDE), 0)
    col = lax.broadcasted_iota(jnp.int32, (16, SIDE), 1)
    wrapped = row * SIDE + col < offset[0]
    earlier = [decode(before_ref, 0), decode(before_ref, 1)]
    before = []
    for comp in (0, 1):
        head = jnp.where(wrapped, after_ref[comp], earlier[0][comp][0:16])
        before.append(jnp.concatenate([head, earlier[0][comp][16:]], axis=0))
    quarters = [
        tuple(before),
        tuple(earlier[1]),
        (own_ref[0, 0:QUARTER, :], own_ref[1, 0:QUARTER, :]),
        (own_ref[0, QUARTER:, :], own_ref[1, QUARTER:, :]),
    ]
    sums, differences = [], []
    for r, pair in enumerate(four_point(quarters, -1)):
        product = from_left(rows_forward[r], jnp.concatenate(pair, axis=0))
        real, imag = times(product[:QUARTER], product[QUARTER:], twist[r, 0], -twist[r, 1])
        ends = [(part[:, :LANES], part[:, LANES:]) for part in (real, imag)]
        sums.append(jnp.concatenate([first + second for first, second in ends], axis=1))
        differences.append(jnp.concatenate([first - second for first, second in ends], axis=1))
    back = []
    for s, inputs in enumerate((sums, differences)):
        product = from_right(jnp.concatenate(inputs, axis=0), columns_forward[s])
        pair = times(product[:, :LANES], product[:, LANES:], response[s, 0], response[s, 1])
        back.append(from_right(jnp.concatenate(pair, axis=1), columns_back[s]))
    ends = back[0] + back[1], back[0] - back[1]
    restored = []
    for r in range(4):
        rows = slice(r * QUARTER, r * QUARTER + QUARTER)
        real = jnp.concatenate([end[rows, :LANES] for end in ends], axis=1)
        imag = jnp.concatenate([end[rows, LANES:] for end in ends], axis=1)
        pair = times(real, imag, twist[r, 0], twist[r, 1])
        product = from_left(rows_back[r], jnp.concatenate(pair, axis=0))
        restored.append((product[:QUARTER], product[QUARTER:]))
    wanted = four_point(restored, 1)[2:]
    scale = 1.0 / NFFT
    real = jnp.concatenate([wanted[0][0], wanted[1][0]], axis=0) * scale
    imag = jnp.concatenate([wanted[0][1], wanted[1][1]], axis=0) * scale
    out_ref[0] = real.astype(BF16)
    out_ref[1] = imag.astype(BF16)

    power = real * real + imag * imag
    row_one = jnp.broadcast_to(jnp.sum(power, axis=1, keepdims=True), (SIDE, LANES))
    row_two = jnp.broadcast_to(jnp.sum(power * power, axis=1, keepdims=True), (SIDE, LANES))
    rows = jnp.concatenate([row_one, row_two], axis=1)
    sums = jnp.dot(
        group[...], rows, preferred_element_type=F32, precision=lax.Precision.HIGHEST
    )
    first_sum, second_sum = sums[:, :LANES], sums[:, LANES:]
    kurtosis = (
        (SKW + 1.0) / (SKW - 1.0) * (SKW * second_sum / (first_sum * first_sum + EPSILON) - 1.0)
    )
    at_row = lax.broadcasted_iota(jnp.int32, (SIDE, 64), 0) // 4
    at_lane = lax.broadcasted_iota(jnp.int32, (SIDE, 64), 1)
    kept = jnp.where(at_row == at_lane, (1 - flags_ref[...]).astype(F32), 0.0)
    weight = jnp.sum(kept, axis=1, keepdims=True) / (1.0 + ((kurtosis - 1.0) / SK_WIDTH) ** 2)
    row = lax.broadcasted_iota(jnp.int32, (SIDE, LANES), 0)
    col = lax.broadcasted_iota(jnp.int32, (SIDE, LANES), 1)
    weight_ref[...] = jnp.sum(jnp.where(row == 4 * col, weight, 0.0), axis=0, keepdims=True)
    value_ref[...] = (
        jnp.concatenate([weight, weight], axis=1) * power
    ).astype(BF16).astype(F32)

    for side in (0, 1):
        bins = bins_ref[pl.ds(side, SIDE, stride=2), :]
        lanes = slice(side * LANES, side * LANES + LANES)
        high_ref[:, lanes] = (bins // LOW_BINS).astype(F32)
        low_ref[:, lanes] = (bins % LOW_BINS).astype(F32)

    per_step = 32
    rows = lax.broadcasted_iota(jnp.int32, (LOW_BINS, SIDE), 0).astype(F32).astype(BF16)
    one, zero = jnp.ones((), BF16), jnp.zeros((), BF16)

    def fold(step, total):
        start = pl.multiple_of(step * per_step, per_step)
        blocks = [
            ref[pl.ds(start, per_step), :] for ref in (high_ref, low_ref, value_ref)
        ]
        spreads, marks = [], []
        for r in range(per_step):
            high, low, value = [
                jnp.broadcast_to(block[r : r + 1], (16, SIDE)).astype(BF16) for block in blocks
            ]
            high = jnp.concatenate([high] * (HIGH_BINS // 16), axis=0)
            value = jnp.concatenate([value] * (HIGH_BINS // 16), axis=0)
            low = jnp.concatenate([low] * (LOW_BINS // 16), axis=0)
            spreads.append(jnp.where(high == rows[:HIGH_BINS], value, zero))
            marks.append(jnp.where(low == rows, one, zero))
        return total + lax.dot_general(
            jnp.concatenate(spreads, axis=1),
            jnp.concatenate(marks, axis=1),
            (((1,), (1,)), ((), ())),
            preferred_element_type=F32,
        )

    total = lax.fori_loop(0, SIDE // per_step, fold, jnp.zeros((HIGH_BINS, LOW_BINS), F32))
    total = total * (BINS / (HALF * N_TM))
    total_ref[...] = jnp.concatenate([total, jnp.zeros_like(total)], axis=1)
    pair = [total_ref[pl.ds(side, N_TM, stride=2), :][:, :LOW_BINS] for side in (0, 1)]
    own = jnp.concatenate(pair, axis=1)
    for channel in range(CHANNELS):
        profile_ref[pl.ds(channel * N_TM, N_TM), :] = own


def filter_and_fold(offset, own, before, after, response, flags, bins, tables):
    vmem = pl.BlockSpec(memory_space=pltpu.VMEM)
    return pl.pallas_call(
        main_body,
        in_specs=[pl.BlockSpec(memory_space=pltpu.SMEM)] + [vmem] * (6 + len(tables)),
        out_shape=(
            jax.ShapeDtypeStruct((2, SIDE, SIDE), BF16),
            jax.ShapeDtypeStruct((1, LANES), F32),
            jax.ShapeDtypeStruct((CHANNELS * N_TM, LANES), F32),
        ),
        scratch_shapes=[pltpu.VMEM((SIDE, SIDE), F32)] * 3
        + [pltpu.VMEM((HIGH_BINS, LANES), F32)],
        compiler_params=pltpu.CompilerParams(vmem_limit_bytes=48 * 1024 * 1024),
        name="filter_and_fold",
    )(offset, own, before, after, response, flags, bins, *tables)


def send(value, down, across):
    return lax.ppermute(value, "tm", steps(down, across))


def on_device(voltages, antenna_gains, chirp_phase, offsets, flags, sample_phase_bins):
    tables = make_tables()
    samples = (
        voltages.reshape(2, 4, TIME_CHUNKS, LANES)
        .transpose(0, 2, 1, 3)
        .reshape(2, TIME_CHUNKS * 4, LANES)
    )
    gains = antenna_gains.transpose(0, 2, 1)
    order = (2, 1, 3, 0)

    def first_send(half, step, value):
        return send(value, step, 0) if half == 0 else send(value, 0, step)

    def second_send(half, step, value):
        return send(value, 0, step) if half == 0 else send(value, step, 0)

    response = make_response(offsets, chirp_phase.reshape(8 * LANES, LANES))
    got = [[], []]
    ready = ()
    for messages in (((0, 2), (1, 2)), ((0, 1), (1, 1), (0, 3), (1, 3)), ((0, 0), (1, 0))):
        made = beamform(gains, samples, messages, ready)
        ready = (made[-1],)
        for (half, step), value in zip(messages, made):
            got[half].append(first_send(half, step, value) if step else value)
    got, response = lax.optimization_barrier((got, response))
    landed = [[], []]
    for half in (0, 1):
        made = middle(got[half], order)
        for step, value in zip(order, made):
            landed[half].append(second_send(half, step, value) if step else value)
    own, ahead, behind = last([landed[half][i] for half in (0, 1) for i in (3, 0, 1, 2)])
    before = lax.ppermute(ahead, "tm", [(s, s + 1) for s in range(N_TM - 1)])
    after = lax.ppermute(behind, "tm", [(s + 1, s) for s in range(N_TM - 1)])

    bins = sample_phase_bins.reshape(512, LANES)
    filtered, weight, partial_profile = filter_and_fold(
        offsets, own, before, after, response, flags, bins, tables
    )
    dedispersed = filtered.reshape(2, 1, HALF)
    sk_weight = weight[:, :64]
    arrived = lax.all_to_all(partial_profile, ("chan", "tm"), 0, 0, tiled=True)
    arrived = arrived.reshape(CHANNELS, N_TM, LANES)
    by_channel = jnp.sum(arrived, axis=1)
    profile = lax.dynamic_slice_in_dim(by_channel, lax.axis_index("chan"), 1, 0)
    band_profile = jnp.sum(by_channel, axis=0)
    return (dedispersed, sk_weight, profile, band_profile)


TIME_CHUNKS = 1048576 // LANES


def solution(mesh):
    placed = (
        P(None, "tm", "chan", None),
        P(None, None, "chan"),
        P("chan", None),
        P("chan"),
        P("chan", "tm"),
        P("tm"),
    )
    return jax.shard_map(
        on_device,
        mesh=mesh,
        in_specs=placed,
        out_specs=(P(None, "chan", "tm"), P("chan", "tm"), P("chan", "tm"), P("tm")),
        check_vma=False,
    )
```

```python
import math

import jax
import jax.numpy as jnp
import ml_dtypes
import numpy as np
from jax import lax
from jax.experimental import pallas as pl
from jax.experimental.pallas import tpu as pltpu
from jax.sharding import PartitionSpec as P

NFFT = 131072
HALF = NFFT // 2
SIDE = 256
OFFSET_BOUND = 4096
SKW = 1024
BINS = 2048
LOW_BINS = 64
HIGH_BINS = BINS // LOW_BINS
SK_WIDTH = 0.05
EPSILON = 1e-06
GRID_SIDE = 4
N_TM = 16
CHANNELS = 8
LANES = 128
QUARTER = 128

F32 = jnp.float32
BF16 = jnp.bfloat16


def split_table(table):
    high = table.astype(np.float32).astype(ml_dtypes.bfloat16)
    low = (table - high.astype(np.float64)).astype(np.float32).astype(ml_dtypes.bfloat16)
    return np.stack([high, low])


def circle(turns, length):
    angle = 2.0 * math.pi / length * (turns % length)
    return np.cos(angle), np.sin(angle)


def real_form(cos, sin):
    return split_table(np.block([[cos, sin], [-sin, cos]]))


def make_tables():
    index = np.arange(QUARTER, dtype=np.int64)
    rows_forward, rows_back, twist = [], [], []
    lanes = np.arange(SIDE, dtype=np.int64)
    for r in range(4):
        cos, sin = circle((4 * index[:, None] + r) * index[None, :], 2 * SIDE)
        rows_forward.append(real_form(cos, sin))
        rows_back.append(real_form(cos.T, -sin.T))
        twist.append(np.stack(circle((4 * index[:, None] + r) * lanes[None, :], NFFT)))
    columns_forward, columns_back = [], []
    for s in range(2):
        cos, sin = circle(index[:, None] * (2 * index[None, :] + s), SIDE)
        columns_forward.append(real_form(cos, -sin))
        columns_back.append(real_form(cos.T, sin.T))
    group = (lanes[:, None] // 4 == lanes[None, :] // 4).astype(np.float32)
    return (
        np.stack(rows_forward),
        np.stack(columns_forward),
        np.stack(columns_back),
        np.stack(rows_back),
        np.stack(twist).astype(np.float32),
        group,
    )


def steps(down, across):
    side = GRID_SIDE
    return [
        (s, (s // side + down) % side * side + (s % side + across) % side)
        for s in range(side * side)
    ]


CODE_TOP = 32000.0
HEADER = 8
ROWS = 2 * 128 + HEADER


def encode(real, imag):
    top = jnp.maximum(jnp.max(jnp.abs(real), axis=0, keepdims=True), jnp.max(jnp.abs(imag), axis=0, keepdims=True))
    top = jnp.broadcast_to(jnp.max(top, axis=1, keepdims=True), (8, SIDE))
    level = jnp.floor(4.0 * jnp.log2(CODE_TOP / jnp.maximum(top, 1e-30)))
    scale = jnp.exp2(0.25 * level)[0:1]
    whole = lambda value: jnp.round(value).astype(jnp.int32).astype(jnp.int16)
    return whole(real * scale), whole(imag * scale), whole(level)


def decode(block_ref, *lead):
    level = block_ref[(*lead, pl.ds(2 * 128, HEADER), slice(None))].astype(jnp.int32).astype(F32)
    step = jnp.exp2(-0.25 * level)[0:1]
    parts = []
    for comp in (0, 1):
        code = block_ref[(*lead, pl.ds(comp * 128, 128), slice(None))]
        parts.append(code.astype(jnp.int32).astype(F32) * step)
    return parts


def beam_body(messages, gains_hbm, samples, *refs):
    table, buffer, planes, gains, arrived = refs[-5:]
    outs = refs[-6 - len(messages) : -6]
    refs[-6][...] = jnp.zeros((8, LANES), F32)
    index = lax.axis_index("tm").astype(jnp.int32)
    down_at = index // GRID_SIDE
    across_at = index % GRID_SIDE

    def copy_of(slot, half, step, j):
        if half == 0:
            rows, cols = down_at + step, across_at + j
        else:
            rows, cols = down_at + j, across_at + step
        block = (rows % GRID_SIDE * GRID_SIDE + cols % GRID_SIDE) * 2 + half
        first = pl.multiple_of(block * 1024, 1024)
        return pltpu.make_async_copy(
            samples.at[:, pl.ds(first, 1024), :], buffer.at[slot], arrived.at[slot]
        )

    fetch = pltpu.make_async_copy(gains_hbm, gains, arrived.at[4 * len(messages)])
    fetch.start()
    copies = []
    for number, (half, step) in enumerate(messages):
        copies.append([copy_of(number * 4 + j, half, step, j) for j in range(4)])
        for copy in copies[-1]:
            copy.start()

    fetch.wait()
    shape = (128, 256)
    row = lax.broadcasted_iota(jnp.int32, shape, 0)
    col = lax.broadcasted_iota(jnp.int32, shape, 1)
    part = row // 64
    imag_out = row // 32 % 2
    slot = row % 32
    chunk = jnp.where(slot < 16, 2 * slot, 2 * (slot - 16) + 1)
    from_imag = col // 128
    source = col % 128 // 4
    antenna = col % 4
    antennas = lax.broadcasted_iota(jnp.int32, (1, 64), 1)
    real = jnp.zeros(shape, F32)
    imag = jnp.zeros(shape, F32)
    for a in range(4):
        own = antennas == index * 4 + a
        pick = lambda comp: jnp.sum(jnp.where(own, gains[comp], 0.0), axis=1, keepdims=True)
        real = jnp.where(antenna == a, pick(0), real)
        imag = jnp.where(antenna == a, pick(1), imag)
    cross = jnp.where(imag_out == 1, imag, -imag)
    value = jnp.where(imag_out == from_imag, real, cross)
    value = jnp.where(chunk == source, value, 0.0)
    high = value.astype(BF16).astype(F32)
    table[...] = jnp.where(part == 0, high, value - high).astype(BF16)

    def combine(at):
        copies[at // 4][at % 4].wait()
        columns = []
        for group in range(8):
            rows = pl.ds(group * 128, 128)
            columns.append(
                jnp.concatenate([buffer[at, 0, rows, :], buffer[at, 1, rows, :]], axis=0)
            )
        product = jnp.dot(
            table[...], jnp.concatenate(columns, axis=1), preferred_element_type=F32
        )
        both = product[:64] + product[64:]
        for comp in (0, 1):
            for side in (0, 1):
                base = comp * 32 + side * 16
                lanes = slice(side * LANES, side * LANES + LANES)
                for group in range(8):
                    rows = pl.ds(group * 16, 16)
                    part = both[base : base + 16, group * 128 : group * 128 + 128]
                    planes[at % 2, comp, rows, lanes] = part

    def finish(at):
        out, j = outs[at // 4], at % 4
        out[j, 0:128], out[j, 128:256], out[j, 256:264] = encode(
            planes[at % 2, 0], planes[at % 2, 1]
        )

    count = 4 * len(messages)
    combine(0)
    for at in range(1, count):
        combine(at)
        finish(at - 1)
    finish(count - 1)


def beamform(gains, samples, messages, ready=()):
    count = len(messages)
    return pl.pallas_call(
        lambda *refs: beam_body(messages, *refs),
        in_specs=[
            pl.BlockSpec(memory_space=pltpu.HBM),
            pl.BlockSpec(memory_space=pltpu.HBM),
        ]
        + [pl.BlockSpec(memory_space=pltpu.VMEM)] * len(ready),
        out_shape=tuple(jax.ShapeDtypeStruct((4, ROWS, SIDE), jnp.int16) for _ in messages)
        + (jax.ShapeDtypeStruct((8, LANES), F32),),
        scratch_shapes=[
            pltpu.VMEM((128, 256), BF16),
            pltpu.VMEM((count * 4, 2, 1024, LANES), BF16),
            pltpu.VMEM((2, 2, 128, SIDE), F32),
            pltpu.VMEM((2, 1, 64), F32),
            pltpu.SemaphoreType.DMA((count * 4 + 1,)),
        ],
        compiler_params=pltpu.CompilerParams(vmem_limit_bytes=50 * 1024 * 1024),
        name="beamform",
    )(gains, samples, *ready)


def middle_body(order, *refs):
    parts, outs = refs[:4], refs[4:]
    for second, out in zip(order, outs):
        total = decode(parts[0], second)
        for part in parts[1:]:
            more = decode(part, second)
            total = [total[0] + more[0], total[1] + more[1]]
        if second:
            out[0:128], out[128:256], out[256:264] = encode(*total)
        else:
            out[0], out[1] = total


def middle(parts, order):
    return pl.pallas_call(
        lambda *refs: middle_body(order, *refs),
        out_shape=tuple(
            jax.ShapeDtypeStruct((ROWS, SIDE), jnp.int16)
            if second
            else jax.ShapeDtypeStruct((2, 128, SIDE), F32)
            for second in order
        ),
        compiler_params=pltpu.CompilerParams(vmem_limit_bytes=16 * 1024 * 1024),
        name="middle",
    )(*parts)


def last_body(*refs):
    parts, (own, ahead, behind) = refs[:8], refs[8:]
    for half in (0, 1):
        mine = parts[half * 4]
        total = [mine[0], mine[1]]
        for part in parts[half * 4 + 1 : half * 4 + 4]:
            more = decode(part)
            total = [total[0] + more[0], total[1] + more[1]]
        rows = pl.ds(half * 128, 128)
        own[0, rows], own[1, rows] = total
        ahead[half, 0:128], ahead[half, 128:256], ahead[half, 256:264] = encode(*total)
        if half == 0:
            behind[0], behind[1] = total[0][0:16], total[1][0:16]


def last(parts):
    return pl.pallas_call(
        last_body,
        out_shape=(
            jax.ShapeDtypeStruct((2, SIDE, SIDE), F32),
            jax.ShapeDtypeStruct((2, ROWS, SIDE), jnp.int16),
            jax.ShapeDtypeStruct((2, 16, SIDE), F32),
        ),
        compiler_params=pltpu.CompilerParams(vmem_limit_bytes=16 * 1024 * 1024),
        name="last",
    )(*parts)


def response_body(offset, phase, out, turned):
    row = lax.broadcasted_iota(jnp.int32, (QUARTER, LANES), 0)
    col = lax.broadcasted_iota(jnp.int32, (QUARTER, LANES), 1)
    for s in (0, 1):
        for part in range(4):
            block = phase[pl.ds(part + 4 * s, LANES, stride=8), :]
            turned[s, pl.ds(part * LANES, LANES), :] = jnp.transpose(block)
        for r in range(4):
            bin_index = 4 * row + r + 512 * (2 * col + s)
            turns = jnp.bitwise_and(bin_index * offset[0], NFFT - 1)
            turns = jnp.where(turns >= HALF, turns - NFFT, turns)
            angle = turned[s, pl.ds(r, QUARTER, stride=4), :]
            angle = angle + turns.astype(F32) * (2.0 * math.pi / NFFT)
            rows = pl.ds(r * QUARTER, QUARTER)
            out[s, 0, rows, :] = jnp.cos(angle)
            out[s, 1, rows, :] = jnp.sin(angle)


def make_response(offset, phase):
    return pl.pallas_call(
        response_body,
        in_specs=[pl.BlockSpec(memory_space=pltpu.SMEM), pl.BlockSpec(memory_space=pltpu.VMEM)],
        out_shape=jax.ShapeDtypeStruct((2, 2, 2 * SIDE, LANES), F32),
        scratch_shapes=[pltpu.VMEM((2, 2 * SIDE, LANES), F32)],
        compiler_params=pltpu.CompilerParams(vmem_limit_bytes=16 * 1024 * 1024),
        name="response",
    )(offset, phase)


def halves(value):
    high = value.astype(BF16)
    return high, (value - high.astype(F32)).astype(BF16)


def from_left(table, value):
    high, low = halves(value)
    first, second = table[0], table[1]
    return (
        jnp.dot(first, high, preferred_element_type=F32)
        + jnp.dot(first, low, preferred_element_type=F32)
        + jnp.dot(second, high, preferred_element_type=F32)
    )


def from_right(value, table):
    high, low = halves(value)
    first, second = table[0], table[1]
    return (
        jnp.dot(high, first, preferred_element_type=F32)
        + jnp.dot(low, first, preferred_element_type=F32)
        + jnp.dot(high, second, preferred_element_type=F32)
    )


def quarter_turn(pair, count):
    real, imag = pair
    return ((real, imag), (-imag, real), (-real, -imag), (imag, -real))[count % 4]


def add(first, second):
    return first[0] + second[0], first[1] + second[1]


def four_point(parts, sign):
    even = add(parts[0], parts[2]), add(parts[1], parts[3])
    odd = add(parts[0], quarter_turn(parts[2], 2)), add(parts[1], quarter_turn(parts[3], 2))
    return (
        add(even[0], even[1]),
        add(odd[0], quarter_turn(odd[1], sign)),
        add(even[0], quarter_turn(even[1], 2)),
        add(odd[0], quarter_turn(odd[1], -sign)),
    )


def times(real, imag, other_real, other_imag):
    return real * other_real - imag * other_imag, real * other_imag + imag * other_real


def main_body(
    offset,
    own_ref,
    before_ref,
    after_ref,
    response,
    flags_ref,
    bins_ref,
    rows_forward,
    columns_forward,
    columns_back,
    rows_back,
    twist,
    group,
    out_ref,
    weight_ref,
    profile_ref,
    high_ref,
    low_ref,
    value_ref,
    total_ref,
):
    own = [own_ref[0], own_ref[1]]
    row = lax.broadcasted_iota(jnp.int32, (16, SIDE), 0)
    col = lax.broadcasted_iota(jnp.int32, (16, SIDE), 1)
    wrapped = row * SIDE + col < offset[0]
    earlier = [decode(before_ref, 0), decode(before_ref, 1)]
    before = []
    for comp in (0, 1):
        head = jnp.where(wrapped, after_ref[comp], earlier[0][comp][0:16])
        before.append(jnp.concatenate([head, earlier[0][comp][16:]], axis=0))
    quarters = [
        tuple(before),
        tuple(earlier[1]),
        (own_ref[0, 0:QUARTER, :], own_ref[1, 0:QUARTER, :]),
        (own_ref[0, QUARTER:, :], own_ref[1, QUARTER:, :]),
    ]
    sums, differences = [], []
    for r, pair in enumerate(four_point(quarters, -1)):
        product = from_left(rows_forward[r], jnp.concatenate(pair, axis=0))
        real, imag = times(product[:QUARTER], product[QUARTER:], twist[r, 0], -twist[r, 1])
        ends = [(part[:, :LANES], part[:, LANES:]) for part in (real, imag)]
        sums.append(jnp.concatenate([first + second for first, second in ends], axis=1))
        differences.append(jnp.concatenate([first - second for first, second in ends], axis=1))
    back = []
    for s, inputs in enumerate((sums, differences)):
        product = from_right(jnp.concatenate(inputs, axis=0), columns_forward[s])
        pair = times(product[:, :LANES], product[:, LANES:], response[s, 0], response[s, 1])
        back.append(from_right(jnp.concatenate(pair, axis=1), columns_back[s]))
    ends = back[0] + back[1], back[0] - back[1]
    restored = []
    for r in range(4):
        rows = slice(r * QUARTER, r * QUARTER + QUARTER)
        real = jnp.concatenate([end[rows, :LANES] for end in ends], axis=1)
        imag = jnp.concatenate([end[rows, LANES:] for end in ends], axis=1)
        pair = times(real, imag, twist[r, 0], twist[r, 1])
        product = from_left(rows_back[r], jnp.concatenate(pair, axis=0))
        restored.append((product[:QUARTER], product[QUARTER:]))
    wanted = four_point(restored, 1)[2:]
    scale = 1.0 / NFFT
    real = jnp.concatenate([wanted[0][0], wanted[1][0]], axis=0) * scale
    imag = jnp.concatenate([wanted[0][1], wanted[1][1]], axis=0) * scale
    out_ref[0] = real.astype(BF16)
    out_ref[1] = imag.astype(BF16)

    power = real * real + imag * imag
    row_one = jnp.broadcast_to(jnp.sum(power, axis=1, keepdims=True), (SIDE, LANES))
    row_two = jnp.broadcast_to(jnp.sum(power * power, axis=1, keepdims=True), (SIDE, LANES))
    rows = jnp.concatenate([row_one, row_two], axis=1)
    sums = jnp.dot(
        group[...], rows, preferred_element_type=F32, precision=lax.Precision.HIGHEST
    )
    first_sum, second_sum = sums[:, :LANES], sums[:, LANES:]
    kurtosis = (
        (SKW + 1.0) / (SKW - 1.0) * (SKW * second_sum / (first_sum * first_sum + EPSILON) - 1.0)
    )
    at_row = lax.broadcasted_iota(jnp.int32, (SIDE, 64), 0) // 4
    at_lane = lax.broadcasted_iota(jnp.int32, (SIDE, 64), 1)
    kept = jnp.where(at_row == at_lane, (1 - flags_ref[...]).astype(F32), 0.0)
    weight = jnp.sum(kept, axis=1, keepdims=True) / (1.0 + ((kurtosis - 1.0) / SK_WIDTH) ** 2)
    row = lax.broadcasted_iota(jnp.int32, (SIDE, LANES), 0)
    col = lax.broadcasted_iota(jnp.int32, (SIDE, LANES), 1)
    weight_ref[...] = jnp.sum(jnp.where(row == 4 * col, weight, 0.0), axis=0, keepdims=True)
    value_ref[...] = (
        jnp.concatenate([weight, weight], axis=1) * power
    ).astype(BF16).astype(F32)

    for side in (0, 1):
        bins = bins_ref[pl.ds(side, SIDE, stride=2), :]
        lanes = slice(side * LANES, side * LANES + LANES)
        high_ref[:, lanes] = (bins // LOW_BINS).astype(F32)
        low_ref[:, lanes] = (bins % LOW_BINS).astype(F32)

    per_step = 32
    rows = lax.broadcasted_iota(jnp.int32, (LOW_BINS, SIDE), 0).astype(F32).astype(BF16)
    one, zero = jnp.ones((), BF16), jnp.zeros((), BF16)

    def fold(step, total):
        start = pl.multiple_of(step * per_step, per_step)
        blocks = [
            ref[pl.ds(start, per_step), :] for ref in (high_ref, low_ref, value_ref)
        ]
        spreads, marks = [], []
        for r in range(per_step):
            high, low, value = [
                jnp.broadcast_to(block[r : r + 1], (16, SIDE)).astype(BF16) for block in blocks
            ]
            high = jnp.concatenate([high] * (HIGH_BINS // 16), axis=0)
            value = jnp.concatenate([value] * (HIGH_BINS // 16), axis=0)
            low = jnp.concatenate([low] * (LOW_BINS // 16), axis=0)
            spreads.append(jnp.where(high == rows[:HIGH_BINS], value, zero))
            marks.append(jnp.where(low == rows, one, zero))
        return total + lax.dot_general(
            jnp.concatenate(spreads, axis=1),
            jnp.concatenate(marks, axis=1),
            (((1,), (1,)), ((), ())),
            preferred_element_type=F32,
        )

    total = lax.fori_loop(0, SIDE // per_step, fold, jnp.zeros((HIGH_BINS, LOW_BINS), F32))
    total = total * (BINS / (HALF * N_TM))
    total_ref[...] = jnp.concatenate([total, jnp.zeros_like(total)], axis=1)
    pair = [total_ref[pl.ds(side, N_TM, stride=2), :][:, :LOW_BINS] for side in (0, 1)]
    own = jnp.concatenate(pair, axis=1)
    for channel in range(CHANNELS):
        profile_ref[pl.ds(channel * N_TM, N_TM), :] = own


def filter_and_fold(offset, own, before, after, response, flags, bins, tables):
    vmem = pl.BlockSpec(memory_space=pltpu.VMEM)
    return pl.pallas_call(
        main_body,
        in_specs=[pl.BlockSpec(memory_space=pltpu.SMEM)] + [vmem] * (6 + len(tables)),
        out_shape=(
            jax.ShapeDtypeStruct((2, SIDE, SIDE), BF16),
            jax.ShapeDtypeStruct((1, LANES), F32),
            jax.ShapeDtypeStruct((CHANNELS * N_TM, LANES), F32),
        ),
        scratch_shapes=[pltpu.VMEM((SIDE, SIDE), F32)] * 3
        + [pltpu.VMEM((HIGH_BINS, LANES), F32)],
        compiler_params=pltpu.CompilerParams(vmem_limit_bytes=48 * 1024 * 1024),
        name="filter_and_fold",
    )(offset, own, before, after, response, flags, bins, *tables)


def send(value, down, across):
    return lax.ppermute(value, "tm", steps(down, across))


def on_device(voltages, antenna_gains, chirp_phase, offsets, flags, sample_phase_bins):
    tables = make_tables()
    samples = (
        voltages.reshape(2, 4, TIME_CHUNKS, LANES)
        .transpose(0, 2, 1, 3)
        .reshape(2, TIME_CHUNKS * 4, LANES)
    )
    gains = antenna_gains.transpose(0, 2, 1)
    order = (2, 1, 3, 0)

    def first_send(half, step, value):
        return send(value, step, 0) if half == 0 else send(value, 0, step)

    def second_send(half, step, value):
        return send(value, 0, step) if half == 0 else send(value, step, 0)

    got = [[], []]
    ready = ()
    for messages in (((0, 2), (1, 2)), ((1, 1), (1, 3), (0, 1), (0, 3)), ((0, 0), (1, 0))):
        if messages[0][1] == 0:
            held = (ready, got[0][0], got[1][0], chirp_phase)
            ready, got[0][0], got[1][0], chirp_phase = lax.optimization_barrier(held)
        made = beamform(gains, samples, messages, ready)
        ready = (made[-1],)
        for (half, step), value in zip(messages, made):
            got[half].append(first_send(half, step, value) if step else value)
    response = make_response(offsets, chirp_phase.reshape(8 * LANES, LANES))
    got, response = lax.optimization_barrier((got, response))
    landed = [[], []]
    for half in (0, 1):
        made = middle(got[half], order)
        for step, value in zip(order, made):
            landed[half].append(second_send(half, step, value) if step else value)
    own, ahead, behind = last([landed[half][i] for half in (0, 1) for i in (3, 0, 1, 2)])
    before = lax.ppermute(ahead, "tm", [(s, s + 1) for s in range(N_TM - 1)])
    after = lax.ppermute(behind, "tm", [(s + 1, s) for s in range(N_TM - 1)])

    bins = sample_phase_bins.reshape(512, LANES)
    filtered, weight, partial_profile = filter_and_fold(
        offsets, own, before, after, response, flags, bins, tables
    )
    dedispersed = filtered.reshape(2, 1, HALF)
    sk_weight = weight[:, :64]
    arrived = lax.all_to_all(partial_profile, ("chan", "tm"), 0, 0, tiled=True)
    by_channel = jnp.sum(arrived.reshape(CHANNELS, N_TM, LANES), axis=1)
    profile = lax.dynamic_slice_in_dim(by_channel, lax.axis_index("chan"), 1, 0)
    band_profile = jnp.sum(by_channel, axis=0)
    return (dedispersed, sk_weight, profile, band_profile)


TIME_CHUNKS = 1048576 // LANES


def solution(mesh):
    placed = (
        P(None, "tm", "chan", None),
        P(None, None, "chan"),
        P("chan", None),
        P("chan"),
        P("chan", "tm"),
        P("tm"),
    )
    return jax.shard_map(
        on_device,
        mesh=mesh,
        in_specs=placed,
        out_specs=(P(None, "chan", "tm"), P("chan", "tm"), P("chan", "tm"), P("tm")),
        check_vma=False,
    )
```

```python
import math

import jax
import jax.numpy as jnp
import ml_dtypes
import numpy as np
from jax import lax
from jax.experimental import pallas as pl
from jax.experimental.pallas import tpu as pltpu
from jax.sharding import PartitionSpec as P

NFFT = 131072
HALF = NFFT // 2
SIDE = 256
OFFSET_BOUND = 4096
SKW = 1024
BINS = 2048
LOW_BINS = 64
HIGH_BINS = BINS // LOW_BINS
SK_WIDTH = 0.05
EPSILON = 1e-06
GRID_SIDE = 4
N_TM = 16
CHANNELS = 8
LANES = 128
QUARTER = 128

F32 = jnp.float32
BF16 = jnp.bfloat16


def split_table(table):
    high = table.astype(np.float32).astype(ml_dtypes.bfloat16)
    low = (table - high.astype(np.float64)).astype(np.float32).astype(ml_dtypes.bfloat16)
    return np.stack([high, low])


def circle(turns, length):
    angle = 2.0 * math.pi / length * (turns % length)
    return np.cos(angle), np.sin(angle)


def real_form(cos, sin):
    return split_table(np.block([[cos, sin], [-sin, cos]]))


def make_tables():
    index = np.arange(QUARTER, dtype=np.int64)
    rows_forward, rows_back, twist = [], [], []
    lanes = np.arange(SIDE, dtype=np.int64)
    for r in range(4):
        cos, sin = circle((4 * index[:, None] + r) * index[None, :], 2 * SIDE)
        rows_forward.append(real_form(cos, sin))
        rows_back.append(real_form(cos.T, -sin.T))
        twist.append(np.stack(circle((4 * index[:, None] + r) * lanes[None, :], NFFT)))
    columns_forward, columns_back = [], []
    for s in range(2):
        cos, sin = circle(index[:, None] * (2 * index[None, :] + s), SIDE)
        columns_forward.append(real_form(cos, -sin))
        columns_back.append(real_form(cos.T, sin.T))
    group = (lanes[:, None] // 4 == lanes[None, :] // 4).astype(np.float32)
    return (
        np.stack(rows_forward),
        np.stack(columns_forward),
        np.stack(columns_back),
        np.stack(rows_back),
        np.stack(twist).astype(np.float32),
        group,
    )


def steps(down, across):
    side = GRID_SIDE
    return [
        (s, (s // side + down) % side * side + (s % side + across) % side)
        for s in range(side * side)
    ]


CODE_TOP = 32000.0
HEADER = 8
ROWS = 2 * 128 + HEADER


def encode(real, imag):
    top = jnp.maximum(jnp.max(jnp.abs(real), axis=0, keepdims=True), jnp.max(jnp.abs(imag), axis=0, keepdims=True))
    top = jnp.broadcast_to(jnp.max(top, axis=1, keepdims=True), (8, SIDE))
    level = jnp.floor(4.0 * jnp.log2(CODE_TOP / jnp.maximum(top, 1e-30)))
    scale = jnp.exp2(0.25 * level)[0:1]
    whole = lambda value: jnp.round(value).astype(jnp.int32).astype(jnp.int16)
    return whole(real * scale), whole(imag * scale), whole(level)


def decode(block_ref, *lead):
    level = block_ref[(*lead, pl.ds(2 * 128, HEADER), slice(None))].astype(jnp.int32).astype(F32)
    step = jnp.exp2(-0.25 * level)[0:1]
    parts = []
    for comp in (0, 1):
        code = block_ref[(*lead, pl.ds(comp * 128, 128), slice(None))]
        parts.append(code.astype(jnp.int32).astype(F32) * step)
    return parts


def beam_body(messages, gains_hbm, samples, *refs):
    table, buffer, planes, gains, arrived = refs[-5:]
    outs = refs[-6 - len(messages) : -6]
    refs[-6][...] = jnp.zeros((8, LANES), F32)
    index = lax.axis_index("tm").astype(jnp.int32)
    down_at = index // GRID_SIDE
    across_at = index % GRID_SIDE

    def copy_of(slot, half, step, j):
        if half == 0:
            rows, cols = down_at + step, across_at + j
        else:
            rows, cols = down_at + j, across_at + step
        block = (rows % GRID_SIDE * GRID_SIDE + cols % GRID_SIDE) * 2 + half
        first = pl.multiple_of(block * 1024, 1024)
        return pltpu.make_async_copy(
            samples.at[:, pl.ds(first, 1024), :], buffer.at[slot], arrived.at[slot]
        )

    fetch = pltpu.make_async_copy(gains_hbm, gains, arrived.at[4 * len(messages)])
    fetch.start()
    copies = []
    for number, (half, step) in enumerate(messages):
        copies.append([copy_of(number * 4 + j, half, step, j) for j in range(4)])
        for copy in copies[-1]:
            copy.start()

    fetch.wait()
    shape = (128, 256)
    row = lax.broadcasted_iota(jnp.int32, shape, 0)
    col = lax.broadcasted_iota(jnp.int32, shape, 1)
    part = row // 64
    imag_out = row // 32 % 2
    slot = row % 32
    chunk = jnp.where(slot < 16, 2 * slot, 2 * (slot - 16) + 1)
    from_imag = col // 128
    source = col % 128 // 4
    antenna = col % 4
    antennas = lax.broadcasted_iota(jnp.int32, (1, 64), 1)
    real = jnp.zeros(shape, F32)
    imag = jnp.zeros(shape, F32)
    for a in range(4):
        own = antennas == index * 4 + a
        pick = lambda comp: jnp.sum(jnp.where(own, gains[comp], 0.0), axis=1, keepdims=True)
        real = jnp.where(antenna == a, pick(0), real)
        imag = jnp.where(antenna == a, pick(1), imag)
    cross = jnp.where(imag_out == 1, imag, -imag)
    value = jnp.where(imag_out == from_imag, real, cross)
    value = jnp.where(chunk == source, value, 0.0)
    high = value.astype(BF16).astype(F32)
    table[...] = jnp.where(part == 0, high, value - high).astype(BF16)

    def combine(at):
        copies[at // 4][at % 4].wait()
        columns = []
        for group in range(8):
            rows = pl.ds(group * 128, 128)
            columns.append(
                jnp.concatenate([buffer[at, 0, rows, :], buffer[at, 1, rows, :]], axis=0)
            )
        product = jnp.dot(
            table[...], jnp.concatenate(columns, axis=1), preferred_element_type=F32
        )
        both = product[:64] + product[64:]
        for comp in (0, 1):
            for side in (0, 1):
                base = comp * 32 + side * 16
                lanes = slice(side * LANES, side * LANES + LANES)
                for group in range(8):
                    rows = pl.ds(group * 16, 16)
                    part = both[base : base + 16, group * 128 : group * 128 + 128]
                    planes[at % 2, comp, rows, lanes] = part

    def finish(at):
        out, j = outs[at // 4], at % 4
        out[j, 0:128], out[j, 128:256], out[j, 256:264] = encode(
            planes[at % 2, 0], planes[at % 2, 1]
        )

    count = 4 * len(messages)
    combine(0)
    for at in range(1, count):
        combine(at)
        finish(at - 1)
    finish(count - 1)


def beamform(gains, samples, messages, ready=()):
    count = len(messages)
    return pl.pallas_call(
        lambda *refs: beam_body(messages, *refs),
        in_specs=[
            pl.BlockSpec(memory_space=pltpu.HBM),
            pl.BlockSpec(memory_space=pltpu.HBM),
        ]
        + [pl.BlockSpec(memory_space=pltpu.VMEM)] * len(ready),
        out_shape=tuple(jax.ShapeDtypeStruct((4, ROWS, SIDE), jnp.int16) for _ in messages)
        + (jax.ShapeDtypeStruct((8, LANES), F32),),
        scratch_shapes=[
            pltpu.VMEM((128, 256), BF16),
            pltpu.VMEM((count * 4, 2, 1024, LANES), BF16),
            pltpu.VMEM((2, 2, 128, SIDE), F32),
            pltpu.VMEM((2, 1, 64), F32),
            pltpu.SemaphoreType.DMA((count * 4 + 1,)),
        ],
        compiler_params=pltpu.CompilerParams(vmem_limit_bytes=50 * 1024 * 1024),
        name="beamform",
    )(gains, samples, *ready)


def middle_body(order, *refs):
    parts, outs = refs[:4], refs[4:]
    for second, out in zip(order, outs):
        total = decode(parts[0], second)
        for part in parts[1:]:
            more = decode(part, second)
            total = [total[0] + more[0], total[1] + more[1]]
        if second:
            out[0:128], out[128:256], out[256:264] = encode(*total)
        else:
            out[0], out[1] = total


def middle(parts, order):
    return pl.pallas_call(
        lambda *refs: middle_body(order, *refs),
        out_shape=tuple(
            jax.ShapeDtypeStruct((ROWS, SIDE), jnp.int16)
            if second
            else jax.ShapeDtypeStruct((2, 128, SIDE), F32)
            for second in order
        ),
        compiler_params=pltpu.CompilerParams(vmem_limit_bytes=16 * 1024 * 1024),
        name="middle",
    )(*parts)


def last_body(*refs):
    parts, outs = refs[:4], refs[4:]
    total = [parts[0][0], parts[0][1]]
    for part in parts[1:]:
        more = decode(part)
        total = [total[0] + more[0], total[1] + more[1]]
    own, ahead = outs[:2]
    own[0], own[1] = total
    ahead[0:128], ahead[128:256], ahead[256:264] = encode(*total)
    if len(outs) > 2:
        outs[2][0], outs[2][1] = total[0][0:16], total[1][0:16]


def last(parts, half):
    behind = (jax.ShapeDtypeStruct((2, 16, SIDE), F32),) if half == 0 else ()
    return pl.pallas_call(
        last_body,
        out_shape=(
            jax.ShapeDtypeStruct((2, 128, SIDE), F32),
            jax.ShapeDtypeStruct((ROWS, SIDE), jnp.int16),
        )
        + behind,
        compiler_params=pltpu.CompilerParams(vmem_limit_bytes=16 * 1024 * 1024),
        name="last",
    )(*parts)


def response_body(offset, phase, out, turned):
    row = lax.broadcasted_iota(jnp.int32, (QUARTER, LANES), 0)
    col = lax.broadcasted_iota(jnp.int32, (QUARTER, LANES), 1)
    for s in (0, 1):
        for part in range(4):
            block = phase[pl.ds(part + 4 * s, LANES, stride=8), :]
            turned[s, pl.ds(part * LANES, LANES), :] = jnp.transpose(block)
        for r in range(4):
            bin_index = 4 * row + r + 512 * (2 * col + s)
            turns = jnp.bitwise_and(bin_index * offset[0], NFFT - 1)
            turns = jnp.where(turns >= HALF, turns - NFFT, turns)
            angle = turned[s, pl.ds(r, QUARTER, stride=4), :]
            angle = angle + turns.astype(F32) * (2.0 * math.pi / NFFT)
            rows = pl.ds(r * QUARTER, QUARTER)
            out[s, 0, rows, :] = jnp.cos(angle)
            out[s, 1, rows, :] = jnp.sin(angle)


def make_response(offset, phase):
    return pl.pallas_call(
        response_body,
        in_specs=[pl.BlockSpec(memory_space=pltpu.SMEM), pl.BlockSpec(memory_space=pltpu.VMEM)],
        out_shape=jax.ShapeDtypeStruct((2, 2, 2 * SIDE, LANES), F32),
        scratch_shapes=[pltpu.VMEM((2, 2 * SIDE, LANES), F32)],
        compiler_params=pltpu.CompilerParams(vmem_limit_bytes=16 * 1024 * 1024),
        name="response",
    )(offset, phase)


def halves(value):
    high = value.astype(BF16)
    return high, (value - high.astype(F32)).astype(BF16)


def from_left(table, value):
    high, low = halves(value)
    first, second = table[0], table[1]
    return (
        jnp.dot(first, high, preferred_element_type=F32)
        + jnp.dot(first, low, preferred_element_type=F32)
        + jnp.dot(second, high, preferred_element_type=F32)
    )


def from_right(value, table):
    high, low = halves(value)
    first, second = table[0], table[1]
    return (
        jnp.dot(high, first, preferred_element_type=F32)
        + jnp.dot(low, first, preferred_element_type=F32)
        + jnp.dot(high, second, preferred_element_type=F32)
    )


def quarter_turn(pair, count):
    real, imag = pair
    return ((real, imag), (-imag, real), (-real, -imag), (imag, -real))[count % 4]


def add(first, second):
    return first[0] + second[0], first[1] + second[1]


def four_point(parts, sign):
    even = add(parts[0], parts[2]), add(parts[1], parts[3])
    odd = add(parts[0], quarter_turn(parts[2], 2)), add(parts[1], quarter_turn(parts[3], 2))
    return (
        add(even[0], even[1]),
        add(odd[0], quarter_turn(odd[1], sign)),
        add(even[0], quarter_turn(even[1], 2)),
        add(odd[0], quarter_turn(odd[1], -sign)),
    )


def times(real, imag, other_real, other_imag):
    return real * other_real - imag * other_imag, real * other_imag + imag * other_real


def main_body(
    offset,
    own_first,
    own_last,
    before_first,
    before_last,
    after_ref,
    response,
    flags_ref,
    high_marks,
    low_marks,
    rows_forward,
    columns_forward,
    columns_back,
    rows_back,
    twist,
    group,
    out_ref,
    weight_ref,
    profile_ref,
    value_ref,
    total_ref,
):
    row = lax.broadcasted_iota(jnp.int32, (16, SIDE), 0)
    col = lax.broadcasted_iota(jnp.int32, (16, SIDE), 1)
    wrapped = row * SIDE + col < offset[0]
    earlier = [decode(before_first), decode(before_last)]
    before = []
    for comp in (0, 1):
        head = jnp.where(wrapped, after_ref[comp], earlier[0][comp][0:16])
        before.append(jnp.concatenate([head, earlier[0][comp][16:]], axis=0))
    quarters = [
        tuple(before),
        tuple(earlier[1]),
        (own_first[0], own_first[1]),
        (own_last[0], own_last[1]),
    ]
    sums, differences = [], []
    for r, pair in enumerate(four_point(quarters, -1)):
        product = from_left(rows_forward[r], jnp.concatenate(pair, axis=0))
        real, imag = times(product[:QUARTER], product[QUARTER:], twist[r, 0], -twist[r, 1])
        ends = [(part[:, :LANES], part[:, LANES:]) for part in (real, imag)]
        sums.append(jnp.concatenate([first + second for first, second in ends], axis=1))
        differences.append(jnp.concatenate([first - second for first, second in ends], axis=1))
    back = []
    for s, inputs in enumerate((sums, differences)):
        product = from_right(jnp.concatenate(inputs, axis=0), columns_forward[s])
        pair = times(product[:, :LANES], product[:, LANES:], response[s, 0], response[s, 1])
        back.append(from_right(jnp.concatenate(pair, axis=1), columns_back[s]))
    ends = back[0] + back[1], back[0] - back[1]
    restored = []
    for r in range(4):
        rows = slice(r * QUARTER, r * QUARTER + QUARTER)
        real = jnp.concatenate([end[rows, :LANES] for end in ends], axis=1)
        imag = jnp.concatenate([end[rows, LANES:] for end in ends], axis=1)
        pair = times(real, imag, twist[r, 0], twist[r, 1])
        product = from_left(rows_back[r], jnp.concatenate(pair, axis=0))
        restored.append((product[:QUARTER], product[QUARTER:]))
    wanted = four_point(restored, 1)[2:]
    scale = 1.0 / NFFT
    real = jnp.concatenate([wanted[0][0], wanted[1][0]], axis=0) * scale
    imag = jnp.concatenate([wanted[0][1], wanted[1][1]], axis=0) * scale
    out_ref[0] = real.astype(BF16)
    out_ref[1] = imag.astype(BF16)

    power = real * real + imag * imag
    row_one = jnp.broadcast_to(jnp.sum(power, axis=1, keepdims=True), (SIDE, LANES))
    row_two = jnp.broadcast_to(jnp.sum(power * power, axis=1, keepdims=True), (SIDE, LANES))
    rows = jnp.concatenate([row_one, row_two], axis=1)
    sums = jnp.dot(
        group[...], rows, preferred_element_type=F32, precision=lax.Precision.HIGHEST
    )
    first_sum, second_sum = sums[:, :LANES], sums[:, LANES:]
    kurtosis = (
        (SKW + 1.0) / (SKW - 1.0) * (SKW * second_sum / (first_sum * first_sum + EPSILON) - 1.0)
    )
    at_row = lax.broadcasted_iota(jnp.int32, (SIDE, 64), 0) // 4
    at_lane = lax.broadcasted_iota(jnp.int32, (SIDE, 64), 1)
    kept = jnp.where(at_row == at_lane, (1 - flags_ref[...]).astype(F32), 0.0)
    weight = jnp.sum(kept, axis=1, keepdims=True) / (1.0 + ((kurtosis - 1.0) / SK_WIDTH) ** 2)
    row = lax.broadcasted_iota(jnp.int32, (SIDE, LANES), 0)
    col = lax.broadcasted_iota(jnp.int32, (SIDE, LANES), 1)
    weight_ref[...] = jnp.sum(jnp.where(row == 4 * col, weight, 0.0), axis=0, keepdims=True)
    value_ref[...] = (
        jnp.concatenate([weight, weight], axis=1) * power
    ).astype(BF16).astype(F32)

    per_step = 64

    def fold(step, total):
        start = pl.multiple_of(step * per_step, per_step)
        block = value_ref[pl.ds(start, per_step), :]
        spreads, marks = [], []
        for r in range(per_step):
            value = jnp.broadcast_to(block[r : r + 1], (16, SIDE)).astype(BF16)
            value = jnp.concatenate([value] * (HIGH_BINS // 16), axis=0)
            spreads.append(high_marks[start + r] * value)
            marks.append(low_marks[start + r])
        return total + lax.dot_general(
            jnp.concatenate(spreads, axis=1),
            jnp.concatenate(marks, axis=1),
            (((1,), (1,)), ((), ())),
            preferred_element_type=F32,
        )

    total = lax.fori_loop(0, SIDE // per_step, fold, jnp.zeros((HIGH_BINS, LOW_BINS), F32))
    total = total * (BINS / (HALF * N_TM))
    total_ref[...] = jnp.concatenate([total, jnp.zeros_like(total)], axis=1)
    pair = [total_ref[pl.ds(side, N_TM, stride=2), :][:, :LOW_BINS] for side in (0, 1)]
    own = jnp.concatenate(pair, axis=1)
    for channel in range(CHANNELS):
        profile_ref[pl.ds(channel * N_TM, N_TM), :] = own


def mark_body(bins_ref, high_marks, low_marks, high_ref, low_ref):
    for side in (0, 1):
        bins = bins_ref[pl.ds(side, SIDE, stride=2), :]
        lanes = slice(side * LANES, side * LANES + LANES)
        high_ref[:, lanes] = (bins // LOW_BINS).astype(F32)
        low_ref[:, lanes] = (bins % LOW_BINS).astype(F32)
    per_step = 16
    rows = lax.broadcasted_iota(jnp.int32, (LOW_BINS, SIDE), 0).astype(F32).astype(BF16)
    one, zero = jnp.ones((), BF16), jnp.zeros((), BF16)

    def mark(step, carry):
        start = pl.multiple_of(step * per_step, per_step)
        for ref, out, count in (
            (high_ref, high_marks, HIGH_BINS),
            (low_ref, low_marks, LOW_BINS),
        ):
            block = ref[pl.ds(start, per_step), :]
            for r in range(per_step):
                wide = jnp.broadcast_to(block[r : r + 1], (16, SIDE)).astype(BF16)
                wide = jnp.concatenate([wide] * (count // 16), axis=0)
                out[start + r] = jnp.where(wide == rows[:count], one, zero)
        return carry

    lax.fori_loop(0, SIDE // per_step, mark, 0)


def mark_bins(bins):
    return pl.pallas_call(
        mark_body,
        out_shape=(
            jax.ShapeDtypeStruct((SIDE, HIGH_BINS, SIDE), BF16),
            jax.ShapeDtypeStruct((SIDE, LOW_BINS, SIDE), BF16),
        ),
        scratch_shapes=[pltpu.VMEM((SIDE, SIDE), F32)] * 2,
        compiler_params=pltpu.CompilerParams(vmem_limit_bytes=16 * 1024 * 1024),
        name="mark_bins",
    )(bins)


def filter_and_fold(offset, own_first, own_last, before_first, before_last, after, response, flags, marks, tables):
    vmem = pl.BlockSpec(memory_space=pltpu.VMEM)
    return pl.pallas_call(
        main_body,
        in_specs=[pl.BlockSpec(memory_space=pltpu.SMEM)] + [vmem] * (9 + len(tables)),
        out_shape=(
            jax.ShapeDtypeStruct((2, SIDE, SIDE), BF16),
            jax.ShapeDtypeStruct((1, LANES), F32),
            jax.ShapeDtypeStruct((CHANNELS * N_TM, LANES), F32),
        ),
        scratch_shapes=[pltpu.VMEM((SIDE, SIDE), F32)]
        + [pltpu.VMEM((HIGH_BINS, LANES), F32)],
        compiler_params=pltpu.CompilerParams(vmem_limit_bytes=20 * 1024 * 1024),
        name="filter_and_fold",
    )(
        offset,
        own_first,
        own_last,
        before_first,
        before_last,
        after,
        response,
        flags,
        *marks,
        *tables,
    )


def send(value, down, across):
    return lax.ppermute(value, "tm", steps(down, across))


def on_device(voltages, antenna_gains, chirp_phase, offsets, flags, sample_phase_bins):
    tables = make_tables()
    samples = (
        voltages.reshape(2, 4, TIME_CHUNKS, LANES)
        .transpose(0, 2, 1, 3)
        .reshape(2, TIME_CHUNKS * 4, LANES)
    )
    gains = antenna_gains.transpose(0, 2, 1)
    order = (2, 1, 3, 0)

    def first_send(half, step, value):
        return send(value, step, 0) if half == 0 else send(value, 0, step)

    def second_send(half, step, value):
        return send(value, 0, step) if half == 0 else send(value, step, 0)

    got = [[], []]
    ready = ()
    for messages in (((0, 2), (1, 2)), ((1, 1), (1, 3), (0, 1), (0, 3)), ((0, 0), (1, 0))):
        if messages[0][1] == 0:
            held = (ready, got[0][0], got[1][0], chirp_phase)
            ready, got[0][0], got[1][0], chirp_phase = lax.optimization_barrier(held)
        made = beamform(gains, samples, messages, ready)
        ready = (made[-1],)
        for (half, step), value in zip(messages, made):
            got[half].append(first_send(half, step, value) if step else value)
    response = make_response(offsets, chirp_phase.reshape(8 * LANES, LANES))
    got, response = lax.optimization_barrier((got, response))
    landed = [[], []]
    for half in (0, 1):
        made = middle(got[half], order)
        for step, value in zip(order, made):
            landed[half].append(second_send(half, step, value) if step else value)
    forward = [(s, s + 1) for s in range(N_TM - 1)]
    own, before = [], []
    for half in (0, 1):
        mine, ahead, *behind = last([landed[half][i] for i in (3, 0, 1, 2)], half)
        own.append(mine)
        before.append(lax.ppermute(ahead, "tm", forward))
        if behind:
            after = lax.ppermute(behind[0], "tm", [(s + 1, s) for s in range(N_TM - 1)])
            landed[1], after = lax.optimization_barrier((landed[1], after))

    marks = mark_bins(sample_phase_bins.reshape(512, LANES))
    filtered, weight, partial_profile = filter_and_fold(
        offsets, *own, *before, after, response, flags, marks, tables
    )
    dedispersed = filtered.reshape(2, 1, HALF)
    sk_weight = weight[:, :64]
    arrived = lax.all_to_all(partial_profile, ("chan", "tm"), 0, 0, tiled=True)
    by_channel = jnp.sum(arrived.reshape(CHANNELS, N_TM, LANES), axis=1)
    profile = lax.dynamic_slice_in_dim(by_channel, lax.axis_index("chan"), 1, 0)
    band_profile = jnp.sum(by_channel, axis=0)
    return (dedispersed, sk_weight, profile, band_profile)


TIME_CHUNKS = 1048576 // LANES


def solution(mesh):
    placed = (
        P(None, "tm", "chan", None),
        P(None, None, "chan"),
        P("chan", None),
        P("chan"),
        P("chan", "tm"),
        P("tm"),
    )
    return jax.shard_map(
        on_device,
        mesh=mesh,
        in_specs=placed,
        out_specs=(P(None, "chan", "tm"), P("chan", "tm"), P("chan", "tm"), P("tm")),
        check_vma=False,
    )
```

```python
import math

import jax
import jax.numpy as jnp
import ml_dtypes
import numpy as np
from jax import lax
from jax.experimental import pallas as pl
from jax.experimental.pallas import tpu as pltpu
from jax.sharding import PartitionSpec as P

NFFT = 131072
HALF = NFFT // 2
SIDE = 256
OFFSET_BOUND = 4096
SKW = 1024
BINS = 2048
LOW_BINS = 64
HIGH_BINS = BINS // LOW_BINS
SK_WIDTH = 0.05
EPSILON = 1e-06
GRID_SIDE = 4
N_TM = 16
CHANNELS = 8
LANES = 128
QUARTER = 128

F32 = jnp.float32
BF16 = jnp.bfloat16


def split_table(table):
    high = table.astype(np.float32).astype(ml_dtypes.bfloat16)
    low = (table - high.astype(np.float64)).astype(np.float32).astype(ml_dtypes.bfloat16)
    return np.stack([high, low])


def circle(turns, length):
    angle = 2.0 * math.pi / length * (turns % length)
    return np.cos(angle), np.sin(angle)


def real_form(cos, sin):
    return split_table(np.block([[cos, sin], [-sin, cos]]))


def make_tables():
    index = np.arange(QUARTER, dtype=np.int64)
    rows_forward, rows_back, twist = [], [], []
    lanes = np.arange(SIDE, dtype=np.int64)
    for r in range(4):
        cos, sin = circle((4 * index[:, None] + r) * index[None, :], 2 * SIDE)
        rows_forward.append(real_form(cos, sin))
        rows_back.append(real_form(cos.T, -sin.T))
        twist.append(np.stack(circle((4 * index[:, None] + r) * lanes[None, :], NFFT)))
    columns_forward, columns_back = [], []
    for s in range(2):
        cos, sin = circle(index[:, None] * (2 * index[None, :] + s), SIDE)
        columns_forward.append(real_form(cos, -sin))
        columns_back.append(real_form(cos.T, sin.T))
    group = (lanes[:, None] // 4 == lanes[None, :] // 4).astype(np.float32)
    return (
        np.stack(rows_forward),
        np.stack(columns_forward),
        np.stack(columns_back),
        np.stack(rows_back),
        np.stack(twist).astype(np.float32),
        group,
    )


def steps(down, across):
    side = GRID_SIDE
    return [
        (s, (s // side + down) % side * side + (s % side + across) % side)
        for s in range(side * side)
    ]


CODE_TOP = 32000.0
HEADER = 8
ROWS = 2 * 128 + HEADER


def encode(real, imag):
    top = jnp.maximum(jnp.max(jnp.abs(real), axis=0, keepdims=True), jnp.max(jnp.abs(imag), axis=0, keepdims=True))
    top = jnp.broadcast_to(jnp.max(top, axis=1, keepdims=True), (8, SIDE))
    level = jnp.floor(4.0 * jnp.log2(CODE_TOP / jnp.maximum(top, 1e-30)))
    scale = jnp.exp2(0.25 * level)[0:1]
    whole = lambda value: jnp.round(value).astype(jnp.int32).astype(jnp.int16)
    return whole(real * scale), whole(imag * scale), whole(level)


def decode(block_ref, *lead):
    level = block_ref[(*lead, pl.ds(2 * 128, HEADER), slice(None))].astype(jnp.int32).astype(F32)
    step = jnp.exp2(-0.25 * level)[0:1]
    parts = []
    for comp in (0, 1):
        code = block_ref[(*lead, pl.ds(comp * 128, 128), slice(None))]
        parts.append(code.astype(jnp.int32).astype(F32) * step)
    return parts


def beam_body(messages, gains_hbm, samples, *refs):
    table, buffer, planes, gains, arrived = refs[-5:]
    outs = refs[-6 - len(messages) : -6]
    refs[-6][...] = jnp.zeros((8, LANES), F32)
    index = lax.axis_index("tm").astype(jnp.int32)
    down_at = index // GRID_SIDE
    across_at = index % GRID_SIDE

    def copy_of(slot, half, step, j):
        if half == 0:
            rows, cols = down_at + step, across_at + j
        else:
            rows, cols = down_at + j, across_at + step
        block = (rows % GRID_SIDE * GRID_SIDE + cols % GRID_SIDE) * 2 + half
        first = pl.multiple_of(block * 1024, 1024)
        return pltpu.make_async_copy(
            samples.at[:, pl.ds(first, 1024), :], buffer.at[slot], arrived.at[slot]
        )

    fetch = pltpu.make_async_copy(gains_hbm, gains, arrived.at[4 * len(messages)])
    fetch.start()
    copies = []
    for number, (half, step) in enumerate(messages):
        copies.append([copy_of(number * 4 + j, half, step, j) for j in range(4)])
        for copy in copies[-1]:
            copy.start()

    fetch.wait()
    shape = (128, 256)
    row = lax.broadcasted_iota(jnp.int32, shape, 0)
    col = lax.broadcasted_iota(jnp.int32, shape, 1)
    part = row // 64
    imag_out = row // 32 % 2
    slot = row % 32
    chunk = jnp.where(slot < 16, 2 * slot, 2 * (slot - 16) + 1)
    from_imag = col // 128
    source = col % 128 // 4
    antenna = col % 4
    antennas = lax.broadcasted_iota(jnp.int32, (1, 64), 1)
    real = jnp.zeros(shape, F32)
    imag = jnp.zeros(shape, F32)
    for a in range(4):
        own = antennas == index * 4 + a
        pick = lambda comp: jnp.sum(jnp.where(own, gains[comp], 0.0), axis=1, keepdims=True)
        real = jnp.where(antenna == a, pick(0), real)
        imag = jnp.where(antenna == a, pick(1), imag)
    cross = jnp.where(imag_out == 1, imag, -imag)
    value = jnp.where(imag_out == from_imag, real, cross)
    value = jnp.where(chunk == source, value, 0.0)
    high = value.astype(BF16).astype(F32)
    table[...] = jnp.where(part == 0, high, value - high).astype(BF16)

    def combine(at):
        copies[at // 4][at % 4].wait()
        columns = []
        for group in range(8):
            rows = pl.ds(group * 128, 128)
            columns.append(
                jnp.concatenate([buffer[at, 0, rows, :], buffer[at, 1, rows, :]], axis=0)
            )
        product = jnp.dot(
            table[...], jnp.concatenate(columns, axis=1), preferred_element_type=F32
        )
        both = product[:64] + product[64:]
        for comp in (0, 1):
            for side in (0, 1):
                base = comp * 32 + side * 16
                lanes = slice(side * LANES, side * LANES + LANES)
                for group in range(8):
                    rows = pl.ds(group * 16, 16)
                    part = both[base : base + 16, group * 128 : group * 128 + 128]
                    planes[at % 2, comp, rows, lanes] = part

    def finish(at):
        out, j = outs[at // 4], at % 4
        out[j, 0:128], out[j, 128:256], out[j, 256:264] = encode(
            planes[at % 2, 0], planes[at % 2, 1]
        )

    count = 4 * len(messages)
    combine(0)
    for at in range(1, count):
        combine(at)
        finish(at - 1)
    finish(count - 1)


def beamform(gains, samples, messages, ready=()):
    count = len(messages)
    return pl.pallas_call(
        lambda *refs: beam_body(messages, *refs),
        in_specs=[
            pl.BlockSpec(memory_space=pltpu.HBM),
            pl.BlockSpec(memory_space=pltpu.HBM),
        ]
        + [pl.BlockSpec(memory_space=pltpu.VMEM)] * len(ready),
        out_shape=tuple(jax.ShapeDtypeStruct((4, ROWS, SIDE), jnp.int16) for _ in messages)
        + (jax.ShapeDtypeStruct((8, LANES), F32),),
        scratch_shapes=[
            pltpu.VMEM((128, 256), BF16),
            pltpu.VMEM((count * 4, 2, 1024, LANES), BF16),
            pltpu.VMEM((2, 2, 128, SIDE), F32),
            pltpu.VMEM((2, 1, 64), F32),
            pltpu.SemaphoreType.DMA((count * 4 + 1,)),
        ],
        compiler_params=pltpu.CompilerParams(vmem_limit_bytes=50 * 1024 * 1024),
        name="beamform",
    )(gains, samples, *ready)


def middle_body(order, *refs):
    parts, outs = refs[:4], refs[4:]
    for second, out in zip(order, outs):
        total = decode(parts[0], second)
        for part in parts[1:]:
            more = decode(part, second)
            total = [total[0] + more[0], total[1] + more[1]]
        if second:
            out[0:128], out[128:256], out[256:264] = encode(*total)
        else:
            out[0], out[1] = total


def middle(parts, order):
    return pl.pallas_call(
        lambda *refs: middle_body(order, *refs),
        out_shape=tuple(
            jax.ShapeDtypeStruct((ROWS, SIDE), jnp.int16)
            if second
            else jax.ShapeDtypeStruct((2, 128, SIDE), F32)
            for second in order
        ),
        compiler_params=pltpu.CompilerParams(vmem_limit_bytes=16 * 1024 * 1024),
        name="middle",
    )(*parts)


def last_body(*refs):
    parts, outs = refs[:4], refs[4:]
    total = [parts[0][0], parts[0][1]]
    for part in parts[1:]:
        more = decode(part)
        total = [total[0] + more[0], total[1] + more[1]]
    own, ahead = outs[:2]
    own[0], own[1] = total
    ahead[0:128], ahead[128:256], ahead[256:264] = encode(*total)
    if len(outs) > 2:
        outs[2][0], outs[2][1] = total[0][0:16], total[1][0:16]


def last(parts, half):
    behind = (jax.ShapeDtypeStruct((2, 16, SIDE), F32),) if half == 0 else ()
    return pl.pallas_call(
        last_body,
        out_shape=(
            jax.ShapeDtypeStruct((2, 128, SIDE), F32),
            jax.ShapeDtypeStruct((ROWS, SIDE), jnp.int16),
        )
        + behind,
        compiler_params=pltpu.CompilerParams(vmem_limit_bytes=16 * 1024 * 1024),
        name="last",
    )(*parts)


def response_body(offset, phase, out, turned):
    row = lax.broadcasted_iota(jnp.int32, (QUARTER, LANES), 0)
    col = lax.broadcasted_iota(jnp.int32, (QUARTER, LANES), 1)
    for s in (0, 1):
        for part in range(4):
            block = phase[pl.ds(part + 4 * s, LANES, stride=8), :]
            turned[s, pl.ds(part * LANES, LANES), :] = jnp.transpose(block)
        for r in range(4):
            bin_index = 4 * row + r + 512 * (2 * col + s)
            turns = jnp.bitwise_and(bin_index * offset[0], NFFT - 1)
            turns = jnp.where(turns >= HALF, turns - NFFT, turns)
            angle = turned[s, pl.ds(r, QUARTER, stride=4), :]
            angle = angle + turns.astype(F32) * (2.0 * math.pi / NFFT)
            rows = pl.ds(r * QUARTER, QUARTER)
            out[s, 0, rows, :] = jnp.cos(angle)
            out[s, 1, rows, :] = jnp.sin(angle)


def make_response(offset, phase):
    return pl.pallas_call(
        response_body,
        in_specs=[pl.BlockSpec(memory_space=pltpu.SMEM), pl.BlockSpec(memory_space=pltpu.VMEM)],
        out_shape=jax.ShapeDtypeStruct((2, 2, 2 * SIDE, LANES), F32),
        scratch_shapes=[pltpu.VMEM((2, 2 * SIDE, LANES), F32)],
        compiler_params=pltpu.CompilerParams(vmem_limit_bytes=16 * 1024 * 1024),
        name="response",
    )(offset, phase)


def halves(value):
    high = value.astype(BF16)
    return high, (value - high.astype(F32)).astype(BF16)


def from_left(table, value):
    high, low = halves(value)
    first, second = table[0], table[1]
    return (
        jnp.dot(first, high, preferred_element_type=F32)
        + jnp.dot(first, low, preferred_element_type=F32)
        + jnp.dot(second, high, preferred_element_type=F32)
    )


def from_right(value, table):
    high, low = halves(value)
    first, second = table[0], table[1]
    return (
        jnp.dot(high, first, preferred_element_type=F32)
        + jnp.dot(low, first, preferred_element_type=F32)
        + jnp.dot(high, second, preferred_element_type=F32)
    )


def quarter_turn(pair, count):
    real, imag = pair
    return ((real, imag), (-imag, real), (-real, -imag), (imag, -real))[count % 4]


def add(first, second):
    return first[0] + second[0], first[1] + second[1]


def four_point(parts, sign):
    even = add(parts[0], parts[2]), add(parts[1], parts[3])
    odd = add(parts[0], quarter_turn(parts[2], 2)), add(parts[1], quarter_turn(parts[3], 2))
    return (
        add(even[0], even[1]),
        add(odd[0], quarter_turn(odd[1], sign)),
        add(even[0], quarter_turn(even[1], 2)),
        add(odd[0], quarter_turn(odd[1], -sign)),
    )


def times(real, imag, other_real, other_imag):
    return real * other_real - imag * other_imag, real * other_imag + imag * other_real


def main_body(
    offset,
    own_first,
    own_last,
    before_first,
    before_last,
    after_ref,
    response,
    flags_ref,
    high_marks,
    low_marks,
    rows_forward,
    columns_forward,
    columns_back,
    rows_back,
    twist,
    group,
    out_ref,
    weight_ref,
    profile_ref,
    value_ref,
    total_ref,
):
    row = lax.broadcasted_iota(jnp.int32, (16, SIDE), 0)
    col = lax.broadcasted_iota(jnp.int32, (16, SIDE), 1)
    wrapped = row * SIDE + col < offset[0]
    earlier = [decode(before_first), decode(before_last)]
    before = []
    for comp in (0, 1):
        head = jnp.where(wrapped, after_ref[comp], earlier[0][comp][0:16])
        before.append(jnp.concatenate([head, earlier[0][comp][16:]], axis=0))
    quarters = [
        tuple(before),
        tuple(earlier[1]),
        (own_first[0], own_first[1]),
        (own_last[0], own_last[1]),
    ]
    sums, differences = [], []
    for r, pair in enumerate(four_point(quarters, -1)):
        product = from_left(rows_forward[r], jnp.concatenate(pair, axis=0))
        real, imag = times(product[:QUARTER], product[QUARTER:], twist[r, 0], -twist[r, 1])
        ends = [(part[:, :LANES], part[:, LANES:]) for part in (real, imag)]
        sums.append(jnp.concatenate([first + second for first, second in ends], axis=1))
        differences.append(jnp.concatenate([first - second for first, second in ends], axis=1))
    back = []
    for s, inputs in enumerate((sums, differences)):
        product = from_right(jnp.concatenate(inputs, axis=0), columns_forward[s])
        pair = times(product[:, :LANES], product[:, LANES:], response[s, 0], response[s, 1])
        back.append(from_right(jnp.concatenate(pair, axis=1), columns_back[s]))
    ends = back[0] + back[1], back[0] - back[1]
    restored = []
    for r in range(4):
        rows = slice(r * QUARTER, r * QUARTER + QUARTER)
        real = jnp.concatenate([end[rows, :LANES] for end in ends], axis=1)
        imag = jnp.concatenate([end[rows, LANES:] for end in ends], axis=1)
        pair = times(real, imag, twist[r, 0], twist[r, 1])
        product = from_left(rows_back[r], jnp.concatenate(pair, axis=0))
        restored.append((product[:QUARTER], product[QUARTER:]))
    wanted = four_point(restored, 1)[2:]
    scale = 1.0 / NFFT
    real = jnp.concatenate([wanted[0][0], wanted[1][0]], axis=0) * scale
    imag = jnp.concatenate([wanted[0][1], wanted[1][1]], axis=0) * scale
    out_ref[0] = real.astype(BF16)
    out_ref[1] = imag.astype(BF16)

    power = real * real + imag * imag
    row_one = jnp.broadcast_to(jnp.sum(power, axis=1, keepdims=True), (SIDE, LANES))
    row_two = jnp.broadcast_to(jnp.sum(power * power, axis=1, keepdims=True), (SIDE, LANES))
    rows = jnp.concatenate([row_one, row_two], axis=1)
    sums = jnp.dot(
        group[...], rows, preferred_element_type=F32, precision=lax.Precision.HIGHEST
    )
    first_sum, second_sum = sums[:, :LANES], sums[:, LANES:]
    kurtosis = (
        (SKW + 1.0) / (SKW - 1.0) * (SKW * second_sum / (first_sum * first_sum + EPSILON) - 1.0)
    )
    at_row = lax.broadcasted_iota(jnp.int32, (SIDE, 64), 0) // 4
    at_lane = lax.broadcasted_iota(jnp.int32, (SIDE, 64), 1)
    kept = jnp.where(at_row == at_lane, (1 - flags_ref[...]).astype(F32), 0.0)
    weight = jnp.sum(kept, axis=1, keepdims=True) / (1.0 + ((kurtosis - 1.0) / SK_WIDTH) ** 2)
    row = lax.broadcasted_iota(jnp.int32, (SIDE, LANES), 0)
    col = lax.broadcasted_iota(jnp.int32, (SIDE, LANES), 1)
    weight_ref[...] = jnp.sum(jnp.where(row == 4 * col, weight, 0.0), axis=0, keepdims=True)
    value_ref[...] = (
        jnp.concatenate([weight, weight], axis=1) * power
    ).astype(BF16).astype(F32)

    per_step = 64

    def fold(step, total):
        start = pl.multiple_of(step * per_step, per_step)
        block = value_ref[pl.ds(start, per_step), :]
        spreads, marks = [], []
        for r in range(per_step):
            value = jnp.broadcast_to(block[r : r + 1], (16, SIDE)).astype(BF16)
            value = jnp.concatenate([value] * (HIGH_BINS // 16), axis=0)
            spreads.append(high_marks[start + r] * value)
            marks.append(low_marks[start + r])
        return total + lax.dot_general(
            jnp.concatenate(spreads, axis=1),
            jnp.concatenate(marks, axis=1),
            (((1,), (1,)), ((), ())),
            preferred_element_type=F32,
        )

    total = lax.fori_loop(0, SIDE // per_step, fold, jnp.zeros((HIGH_BINS, LOW_BINS), F32))
    total = total * (BINS / (HALF * N_TM))
    total_ref[...] = jnp.concatenate([total, jnp.zeros_like(total)], axis=1)
    pair = [total_ref[pl.ds(side, N_TM, stride=2), :][:, :LOW_BINS] for side in (0, 1)]
    own = jnp.concatenate(pair, axis=1)
    for shard in range(N_TM):
        profile_ref[pl.ds(shard * CHANNELS, CHANNELS), :] = jnp.broadcast_to(
            own[shard : shard + 1], (CHANNELS, LANES)
        )


def mark_body(bins_ref, high_marks, low_marks, high_ref, low_ref):
    for side in (0, 1):
        bins = bins_ref[pl.ds(side, SIDE, stride=2), :]
        lanes = slice(side * LANES, side * LANES + LANES)
        high_ref[:, lanes] = (bins // LOW_BINS).astype(F32)
        low_ref[:, lanes] = (bins % LOW_BINS).astype(F32)
    per_step = 16
    rows = lax.broadcasted_iota(jnp.int32, (LOW_BINS, SIDE), 0).astype(F32).astype(BF16)
    one, zero = jnp.ones((), BF16), jnp.zeros((), BF16)

    def mark(step, carry):
        start = pl.multiple_of(step * per_step, per_step)
        for ref, out, count in (
            (high_ref, high_marks, HIGH_BINS),
            (low_ref, low_marks, LOW_BINS),
        ):
            block = ref[pl.ds(start, per_step), :]
            for r in range(per_step):
                wide = jnp.broadcast_to(block[r : r + 1], (16, SIDE)).astype(BF16)
                wide = jnp.concatenate([wide] * (count // 16), axis=0)
                out[start + r] = jnp.where(wide == rows[:count], one, zero)
        return carry

    lax.fori_loop(0, SIDE // per_step, mark, 0)


def mark_bins(bins):
    return pl.pallas_call(
        mark_body,
        out_shape=(
            jax.ShapeDtypeStruct((SIDE, HIGH_BINS, SIDE), BF16),
            jax.ShapeDtypeStruct((SIDE, LOW_BINS, SIDE), BF16),
        ),
        scratch_shapes=[pltpu.VMEM((SIDE, SIDE), F32)] * 2,
        compiler_params=pltpu.CompilerParams(vmem_limit_bytes=16 * 1024 * 1024),
        name="mark_bins",
    )(bins)


def filter_and_fold(offset, own_first, own_last, before_first, before_last, after, response, flags, marks, tables):
    vmem = pl.BlockSpec(memory_space=pltpu.VMEM)
    return pl.pallas_call(
        main_body,
        in_specs=[pl.BlockSpec(memory_space=pltpu.SMEM)] + [vmem] * (9 + len(tables)),
        out_shape=(
            jax.ShapeDtypeStruct((2, SIDE, SIDE), BF16),
            jax.ShapeDtypeStruct((1, LANES), F32),
            jax.ShapeDtypeStruct((CHANNELS * N_TM, LANES), F32),
        ),
        scratch_shapes=[pltpu.VMEM((SIDE, SIDE), F32)]
        + [pltpu.VMEM((HIGH_BINS, LANES), F32)],
        compiler_params=pltpu.CompilerParams(vmem_limit_bytes=20 * 1024 * 1024),
        name="filter_and_fold",
    )(
        offset,
        own_first,
        own_last,
        before_first,
        before_last,
        after,
        response,
        flags,
        *marks,
        *tables,
    )


def send(value, down, across):
    return lax.ppermute(value, "tm", steps(down, across))


def on_device(voltages, antenna_gains, chirp_phase, offsets, flags, sample_phase_bins):
    tables = make_tables()
    samples = (
        voltages.reshape(2, 4, TIME_CHUNKS, LANES)
        .transpose(0, 2, 1, 3)
        .reshape(2, TIME_CHUNKS * 4, LANES)
    )
    gains = antenna_gains.transpose(0, 2, 1)
    order = (1, 3, 2, 0)

    def first_send(half, step, value):
        return send(value, step, 0) if half == 0 else send(value, 0, step)

    def second_send(half, step, value):
        return send(value, 0, step) if half == 0 else send(value, step, 0)

    got = [[], []]
    ready = ()
    for messages in (((0, 2), (1, 2)), ((1, 1), (1, 3), (0, 1), (0, 3)), ((0, 0), (1, 0))):
        if messages[0][1] == 0:
            held = (ready, got[0][0], got[1][0], chirp_phase)
            ready, got[0][0], got[1][0], chirp_phase = lax.optimization_barrier(held)
        made = beamform(gains, samples, messages, ready)
        ready = (made[-1],)
        for (half, step), value in zip(messages, made):
            got[half].append(first_send(half, step, value) if step else value)
    response = make_response(offsets, chirp_phase.reshape(8 * LANES, LANES))
    got, response = lax.optimization_barrier((got, response))
    landed = [[], []]
    for half in (0, 1):
        made = middle(got[half], order)
        for step, value in zip(order, made):
            landed[half].append(second_send(half, step, value) if step else value)
    forward = [(s, s + 1) for s in range(N_TM - 1)]
    own, before = [], []
    for half in (0, 1):
        mine, ahead, *behind = last([landed[half][i] for i in (3, 0, 1, 2)], half)
        own.append(mine)
        before.append(lax.ppermute(ahead, "tm", forward))
        if behind:
            after = lax.ppermute(behind[0], "tm", [(s + 1, s) for s in range(N_TM - 1)])
            landed[1], after = lax.optimization_barrier((landed[1], after))

    marks = mark_bins(sample_phase_bins.reshape(512, LANES))
    filtered, weight, partial_profile = filter_and_fold(
        offsets, *own, *before, after, response, flags, marks, tables
    )
    dedispersed = filtered.reshape(2, 1, HALF)
    sk_weight = weight[:, :64]
    arrived = lax.all_to_all(partial_profile, ("tm", "chan"), 0, 0, tiled=True)
    by_channel = jnp.sum(arrived.reshape(N_TM, CHANNELS, LANES), axis=0)
    profile = lax.dynamic_slice_in_dim(by_channel, lax.axis_index("chan"), 1, 0)
    band_profile = jnp.sum(by_channel, axis=0)
    return (dedispersed, sk_weight, profile, band_profile)


TIME_CHUNKS = 1048576 // LANES


def solution(mesh):
    placed = (
        P(None, "tm", "chan", None),
        P(None, None, "chan"),
        P("chan", None),
        P("chan"),
        P("chan", "tm"),
        P("tm"),
    )
    return jax.shard_map(
        on_device,
        mesh=mesh,
        in_specs=placed,
        out_specs=(P(None, "chan", "tm"), P("chan", "tm"), P("chan", "tm"), P("tm")),
        check_vma=False,
    )
```
